512 devices in a mesh: gx: 128 (over y_lo, x, z), gy: 4 (over y_hi, core).
Axes of the slice: x: 4, y: 4 (y_hi: 2, y_lo: 2; y = y_hi * 2 + y_lo), z: 16, core: 2. Of those that a mesh axis runs over, the one named last changes fastest.
Arguments:
- features: bfloat16 [262144, 128], P(('gx', 'gy')), may hold values from -6 to 6
- cotangent: bfloat16 [262144, 128], P(('gx', 'gy')), may hold values from -6 to 6
- block_pos: int32 [4096], P(('gx', 'gy')), may hold values from -1 to 11, as said below
- weight_one: bfloat16 [3456, 128], replicated, may hold values from -0.1875 to 0.1875
- weight_two: bfloat16 [3456, 128], replicated, may hold values from -0.1875 to 0.1875
Outputs:
- output: bfloat16 [262144, 128], P(('gx', 'gy'))
- input_grad: float32 [262144, 128], P(('gx', 'gy'))
- grad_one: float32 [3456, 128], replicated
- grad_two: float32 [3456, 128], replicated
The draws below stay inside these ranges and needn't reach their ends.
Inputs may be any that keep to these rules, and one draw needn't show every extreme that they name: `block_pos`: local position p numbers a device's 2 x 2 x 3 block grid as (bx * 2 + by) * 3 + bz. A device's used slots come first and hold distinct positions, the rest hold -1; every device uses 2 or more slots and some device uses all 8.
All inputs are finite; a program needn't handle non-finite values.
Results may differ from the reference program's by a relative error of at most 0.0043.
Values may be sent and summed in bfloat16 or wider, within the bound.
No kernel may reach another device: no remote copies, remote signals or barrier semaphores. Data moves between devices by JAX's collectives and lax.ppermute only.
A program may use at most 128 MiB of HBM per device.

```python
import jax
import jax.numpy as jnp
from jax import lax

C = 128
LBX = 2
LBY = 2
LBZ = 3
POS = 12
NB = 8
NBX = 256
NBY = 8
ROWS = 262144
N_GX = 128
N_GY = 4


def draw_block_pos(key, part):
    dev_count = N_GX * N_GY
    perm_key, count_key, full_key = jax.random.split(key, 3)
    orders = jax.vmap(lambda sub_key: jax.random.permutation(sub_key, POS))(jax.random.split(perm_key, dev_count))
    orders = orders.astype(jnp.int32)
    counts = jax.random.randint(count_key, (dev_count,), NB // 4, NB + 1)
    fullest = jax.random.randint(full_key, (), 0, dev_count)
    devices = jnp.arange(dev_count)
    counts = jnp.where(devices == fullest, NB, counts)
    first_at = jnp.argmax(orders == POS - 1, axis=1).astype(jnp.int32)
    rolled = jnp.take_along_axis(orders, (jnp.arange(POS, dtype=jnp.int32)[None, :] + first_at[:, None]) % POS, axis=1)
    orders = jnp.where((devices == fullest)[:, None], rolled, orders)
    chosen = jnp.where(jnp.arange(NB)[None, :] < counts[:, None], orders[:, :NB], -1)
    return chosen.reshape(-1).astype(jnp.int32)


def shard_levels(stream_key, dims, cuts, smallest, top_value):
    loudness = 1.0
    for dim, shards_of in cuts:
        steps = jax.random.uniform(jax.random.fold_in(jax.random.fold_in(stream_key, 6), dim), (shards_of,), jnp.float32, smallest / len(cuts), top_value / len(cuts))
        loudness = loudness * jnp.repeat(jnp.exp(steps), dims[dim] // shards_of).reshape((-1,) + (1,) * (len(dims) - 1 - dim))
    return loudness


def bell_draw(stream_key, dims, deviation, limit, cuts=(), kind=jnp.bfloat16):
    array = deviation * jax.random.normal(stream_key, dims, jnp.float32)
    if cuts:
        array = array * shard_levels(stream_key, dims, cuts, -0.22, 0.18)
    return jnp.clip(array, -limit, limit).astype(kind)


def setup_inputs(seed: int = 0) -> dict:
    key_of = jax.random.split(jax.random.key(seed), 6)
    return {
        "features": bell_draw(key_of[0], (ROWS, C), 1.0, 6.0, ((0, 512),)),
        "cotangent": bell_draw(key_of[1], (ROWS, C), 1.0, 6.0, ((0, 512),)),
        "block_pos": draw_block_pos(jax.random.fold_in(key_of[5], 71), 0),
        "weight_one": bell_draw(key_of[3], (27 * C, C), (9 * C) ** -0.5, 0.1875),
        "weight_two": bell_draw(key_of[4], (27 * C, C), (9 * C) ** -0.5, 0.1875),
    }


def flipped(weight):
    width = weight.shape[1]
    return weight.reshape(27, width, width)[::-1].transpose(0, 2, 1).reshape(27 * width, width)

def columns_of(padded, corner_x, corner_y, corner_z):
    chan_width = padded.shape[3]

    def window(start_x, start_y, start_z):
        starts = (start_x.astype(jnp.int32), start_y.astype(jnp.int32), start_z.astype(jnp.int32), jnp.zeros((), jnp.int32))
        return lax.dynamic_slice(padded, starts, (6, 6, 6, chan_width))
    windows = jax.vmap(window)(corner_x, corner_y, corner_z)
    pieces = [windows[:, off_x:off_x + 4, off_y:off_y + 4, off_z:off_z + 4] for off_x in range(3) for off_y in range(3) for off_z in range(3)]
    stacked = jnp.stack(pieces, axis=4)
    return stacked.reshape(windows.shape[0] * 64, 27 * chan_width)

def reference(features, cotangent, block_pos, weight_one, weight_two):
    chan_width = features.shape[1]
    dev_count = N_GX * N_GY
    active = block_pos >= 0
    row_mask = jnp.repeat(active, 64)[:, None]
    slot_ids = jnp.arange(dev_count * NB, dtype=jnp.int32)
    device = slot_ids // NB
    index_x = device // N_GY
    index_y = device % N_GY
    position = jnp.where(active, block_pos, 0).astype(jnp.int32)
    block_x = index_x * LBX + position // (LBY * LBZ)
    block_y = index_y * LBY + position // LBZ % LBY
    block_z = position % LBZ
    flat = jnp.where(active, (block_x * NBY + block_y) * LBZ + block_z, NBX * NBY * LBZ).astype(jnp.int32)
    corner_x = (block_x * 4).astype(jnp.int32).reshape(dev_count, NB)
    corner_y = (block_y * 4).astype(jnp.int32).reshape(dev_count, NB)
    corner_z = (block_z * 4).astype(jnp.int32).reshape(dev_count, NB)

    def to_dense(values):
        blocks = jnp.zeros((NBX * NBY * LBZ, 64 * chan_width), values.dtype)
        blocks = blocks.at[flat].set(values.reshape(-1, 64 * chan_width), mode='drop')
        blocks = blocks.reshape(NBX, NBY, LBZ, 4, 4, 4, chan_width).transpose(0, 3, 1, 4, 2, 5, 6)
        dense = blocks.reshape(NBX * 4, NBY * 4, LBZ * 4, chan_width)
        return jnp.pad(dense, ((1, 1), (1, 1), (1, 1), (0, 0)))

    def conv_all(values, weight):
        padded = to_dense(values)

        def per_device(corners):
            cols = columns_of(padded, corners[0], corners[1], corners[2])
            return jnp.dot(cols, weight, preferred_element_type=jnp.float32)
        result = lax.map(per_device, (corner_x, corner_y, corner_z))
        return result.reshape(-1, chan_width)

    def gram_all(values, grads):
        padded = to_dense(values)
        grads_dev = grads.reshape(dev_count, NB * 64, chan_width)

        def step_fn(carry, item):
            corners_x, corners_y, corners_z, grad_rows = item
            cols = columns_of(padded, corners_x, corners_y, corners_z)
            term = lax.dot_general(cols, grad_rows, (((0,), (0,)), ((), ())), preferred_element_type=jnp.float32)
            return (carry + term, None)
        start = jnp.zeros((27 * chan_width, chan_width), jnp.float32)
        total, _ = lax.scan(step_fn, start, (corner_x, corner_y, corner_z, grads_dev))
        return total / jnp.sqrt(jnp.float32(ROWS))
    x_in = jnp.where(row_mask, features, 0).astype(jnp.bfloat16)
    pre_one = conv_all(x_in, weight_one)
    sigmoid_one = jax.nn.sigmoid(pre_one)
    hidden = jnp.where(row_mask, pre_one * sigmoid_one, 0.0).astype(jnp.bfloat16)
    pre_two = conv_all(hidden, weight_two)
    output = jnp.where(row_mask, pre_two + x_in.astype(jnp.float32), 0.0).astype(jnp.bfloat16)
    upstream = jnp.where(row_mask, cotangent, 0).astype(jnp.bfloat16)
    back_two = conv_all(upstream, flipped(weight_two))
    slope = sigmoid_one * (1.0 + pre_one * (1.0 - sigmoid_one))
    hidden_grad = jnp.where(row_mask, back_two * slope, 0.0).astype(jnp.bfloat16)
    back_one = conv_all(hidden_grad, flipped(weight_one))
    input_grad = jnp.where(row_mask, upstream.astype(jnp.float32) + back_one, 0.0).astype(jnp.float32)
    grad_two = gram_all(hidden, upstream)
    grad_one = gram_all(x_in, hidden_grad)
    return (output, input_grad, grad_one, grad_two)
```

```python
import jax
import jax.numpy as jnp
from jax import lax
from jax.experimental import pallas as pl
from jax.experimental.pallas import tpu as pltpu
from jax.sharding import Mesh
from jax.sharding import PartitionSpec as P

LBY, LBZ = 2, 3
SLOTS = 8
C = 128
GX, GY, GZ = 8, 8, 16
PX, PY = GX + 2, GY + 2
ROWS = GX * GY * GZ
PAD_ROWS = PX * PY * GZ
DIMS = (2, 4, 4, 4, 2, 2)
NAMES = ("y_lo", "x", "z_hi", "z_lo", "y_hi", "core")
INTERPRET = False
BF = jnp.bfloat16
F32 = jnp.float32


def grid_row(pos_ref, index):
    slot = index >> 6
    pos = jnp.full(index.shape, -1, jnp.int32)
    for s in range(SLOTS):
        pos = jnp.where(slot == s, pos_ref[s], pos)
    safe = jnp.maximum(pos, 0)
    bx = (safe >= 6).astype(jnp.int32)
    rest = safe - 6 * bx
    by = (rest >= 3).astype(jnp.int32)
    bz = rest - 3 * by
    vx = (index >> 4) & 3
    vy = (index >> 2) & 3
    vz = index & 3
    row = ((bx * 4 + vx) * GY + by * 4 + vy) * GZ + bz * 4 + vz
    return jnp.where(pos >= 0, row, -1)


def dot(a, b, dims=((1,), (0,))):
    return lax.dot_general(a, b, (dims, ((), ())), preferred_element_type=F32)


def place_kernel(pos_ref, feat_ref, cot_ref, grid_ref, lo_ref, hi_ref):
    target = grid_row(pos_ref, lax.broadcasted_iota(jnp.int32, (1, SLOTS * 64), 1))
    rows = lax.broadcasted_iota(jnp.int32, (ROWS, SLOTS * 64), 0)
    perm = (rows == target).astype(F32).astype(BF)
    for field, ref in enumerate((feat_ref, cot_ref)):
        placed = dot(perm, ref[...]).astype(BF)
        grid_ref[field] = placed
        lo_ref[field] = placed[: GY * GZ]
        hi_ref[field] = placed[ROWS - GY * GZ :]
    grid_ref[2] = dot(perm, jnp.ones((SLOTS * 64, C), BF)).astype(BF)


def z_shifts(field):
    rows = field.shape[0]
    wide = field.astype(F32)
    before = pltpu.roll(wide, 1, 0).astype(BF)
    after = pltpu.roll(wide, rows - 1, 0).astype(BF)
    return jnp.concatenate([before, field, after], axis=1)


def fill_pad(pad_ref, grid, x_lo, x_hi, y_lo, y_hi):
    pad_ref[1 : PX - 1, 1 : PY - 1] = grid.reshape(GX, GY, GZ, C)
    pad_ref[0, 1 : PY - 1] = x_lo.reshape(GY, GZ, C)
    pad_ref[PX - 1, 1 : PY - 1] = x_hi.reshape(GY, GZ, C)
    pad_ref[:, 0] = y_lo.reshape(PX, GZ, C)
    pad_ref[:, PY - 1] = y_hi.reshape(PX, GZ, C)


def conv(shift_ref, w_ref):
    acc = None
    for k in range(9):
        dx, dy = divmod(k, 3)
        lhs = shift_ref[dx : dx + GX, dy : dy + GY].reshape(ROWS, 3 * C)
        term = dot(lhs, w_ref[k * 3 * C : (k + 1) * 3 * C, :])
        acc = term if acc is None else acc + term
    return acc


def middle_kernel(
    scale, grid_ref, xlo_ref, xhi_ref, ylo_ref, yhi_ref, w1_ref, w2f_ref,
    fields_ref, lo_ref, hi_ref, term1_ref, term2_ref, padx_ref, padu_ref, shift_ref, pre_ref,
):
    mask = grid_ref[2].astype(F32)
    fill_pad(padx_ref, grid_ref[0], xlo_ref[0], xhi_ref[0], ylo_ref[0], yhi_ref[0])
    fill_pad(padu_ref, grid_ref[1], xlo_ref[1], xhi_ref[1], ylo_ref[1], yhi_ref[1])
    shift_ref[...] = z_shifts(padx_ref[...].reshape(PAD_ROWS, C)).reshape(PX, PY, GZ, 3 * C)
    pre_ref[...] = conv(shift_ref, w1_ref)
    shift_ref[...] = z_shifts(padu_ref[...].reshape(PAD_ROWS, C)).reshape(PX, PY, GZ, 3 * C)
    back = conv(shift_ref, w2f_ref)
    pre = pre_ref[...]
    sig = jax.nn.sigmoid(pre)
    hidden = (pre * sig * mask).astype(BF)
    hgrad = (back * (sig * (1.0 + pre * (1.0 - sig))) * mask).astype(BF)
    fields_ref[0] = hidden
    fields_ref[1] = hgrad
    for field, value in enumerate((hidden, hgrad)):
        lo_ref[field] = value[: GY * GZ]
        hi_ref[field] = value[ROWS - GY * GZ :]
    hz = z_shifts(hidden).T
    for k in range(9):
        dx, dy = divmod(k, 3)
        rhs = padu_ref[2 - dx : 2 - dx + GX, 2 - dy : 2 - dy + GY].reshape(ROWS, C)
        term2_ref[k * 3 * C : (k + 1) * 3 * C, :] = (dot(hz, rhs) * scale).astype(term2_ref.dtype)
    gz = z_shifts(hgrad).T
    for k in range(9):
        dx, dy = divmod(k, 3)
        rhs = padx_ref[dx : dx + GX, dy : dy + GY].reshape(ROWS, C)
        prod = dot(gz, rhs) * scale
        for oz in range(3):
            block = prod[(2 - oz) * C : (3 - oz) * C, :].T
            term1_ref[(3 * k + oz) * C : (3 * k + oz + 1) * C, :] = block.astype(term1_ref.dtype)


def final_kernel(
    pos_ref, grid_ref, fields_ref, xlo_ref, xhi_ref, ylo_ref, yhi_ref, w2_ref, w1f_ref,
    out_ref, grad_ref, pad_ref, shift_ref,
):
    target = grid_row(pos_ref, lax.broadcasted_iota(jnp.int32, (SLOTS * 64, 1), 0))
    rows = lax.broadcasted_iota(jnp.int32, (SLOTS * 64, ROWS), 1)
    perm = (rows == target).astype(F32).astype(BF)
    for field, w_ref in enumerate((w2_ref, w1f_ref)):
        fill_pad(pad_ref, fields_ref[field], xlo_ref[field], xhi_ref[field], ylo_ref[field], yhi_ref[field])
        shift_ref[...] = z_shifts(pad_ref[...].reshape(PAD_ROWS, C)).reshape(PX, PY, GZ, 3 * C)
        value = conv(shift_ref, w_ref) + grid_ref[field].astype(F32)
        high = value.astype(BF)
        if field == 0:
            out_ref[...] = dot(perm, high).astype(BF)
        else:
            low = (value - high.astype(F32)).astype(BF)
            grad_ref[...] = dot(perm, high) + dot(perm, low)


def call(kernel, outs, scratch=(), smem=0, args=()):
    specs = [pl.BlockSpec(memory_space=pltpu.SMEM)] * smem
    specs += [pl.BlockSpec(memory_space=pltpu.VMEM)] * (len(args) - smem)
    return pl.pallas_call(
        kernel,
        out_shape=outs,
        in_specs=specs,
        out_specs=jax.tree.map(lambda _: pl.BlockSpec(memory_space=pltpu.VMEM), outs),
        scratch_shapes=list(scratch),
        compiler_params=pltpu.CompilerParams(vmem_limit_bytes=56 << 20),
        interpret=INTERPRET,
    )(*args)


def flipped(weight):
    return weight.reshape(27, C, C)[::-1].transpose(0, 2, 1).reshape(27 * C, C)


def ring(axes):
    count = lax.axis_size(axes)
    forward = [(i, i + 1) for i in range(count - 1)]
    return forward, [(b, a) for a, b in forward]


GXN = ("y_lo", "x", "z_hi", "z_lo")
GYN = ("y_hi", "core")


def exchange(fields, lo, hi):
    forward, backward = ring(GXN)
    x_lo = lax.ppermute(hi, GXN, forward)
    x_hi = lax.ppermute(lo, GXN, backward)
    grid = fields.reshape(-1, GX, GY, GZ, C)[:2]
    lows = x_lo.reshape(2, 1, GY, GZ, C)
    highs = x_hi.reshape(2, 1, GY, GZ, C)

    def face(y):
        return jnp.concatenate([lows[:, :, y], grid[:, :, y], highs[:, :, y]], axis=1).reshape(2, PX * GZ, C)

    forward, backward = ring(GYN)
    y_lo = lax.ppermute(face(GY - 1), GYN, forward)
    y_hi = lax.ppermute(face(0), GYN, backward)
    return x_lo, x_hi, y_lo, y_hi


def scatter_sum(values, axes):
    count = lax.axis_size(axes)
    pieces = lax.all_to_all(values, axes, 0, 0, tiled=True)
    return pieces.reshape(count, -1, C).astype(F32).sum(axis=0)


def group_sum(values, axis):
    count = lax.axis_size(axis)
    got = [lax.ppermute(values, axis, [(i, i ^ d) for i in range(count)]) for d in range(1, count)]
    if count == 1:
        return values
    if count == 2:
        return values + got[0]
    return (values + got[1]) + (got[0] + got[2])


def reduce_terms(terms):
    share = scatter_sum(terms, "core").astype(BF)
    share = scatter_sum(share, ("y_hi", "y_lo", "x"))
    rows = share.shape[0]
    padded = -(-rows // (8 * lax.axis_size("z_lo"))) * 8 * lax.axis_size("z_lo")
    share = jnp.pad(share, ((0, padded - rows), (0, 0)))
    share = group_sum(scatter_sum(share, "z_lo"), "z_hi").astype(BF)
    share = lax.all_gather(share, "z_lo", tiled=True)[:rows]
    share = lax.all_gather(share, "x", tiled=True)
    share = lax.all_gather(share, ("y_hi", "y_lo"), tiled=True)
    other = lax.ppermute(share, "core", [(0, 1), (1, 0)])
    first = lax.axis_index("core") == 0
    return jnp.where(first, share, other).astype(F32), jnp.where(first, other, share).astype(F32)


def per_device(features, cotangent, block_pos, weight_one, weight_two):
    total_rows = block_pos.shape[0] * 64 * lax.axis_size(NAMES)
    scale = float(total_rows) ** -0.5
    grid_shape = jax.ShapeDtypeStruct((3, ROWS, C), BF)
    face_shape = jax.ShapeDtypeStruct((2, GY * GZ, C), BF)
    fields_shape = jax.ShapeDtypeStruct((2, ROWS, C), BF)
    pad = pltpu.VMEM((PX, PY, GZ, C), BF)
    shifts = pltpu.VMEM((PX, PY, GZ, 3 * C), BF)
    grid, lo, hi = call(
        place_kernel, (grid_shape, face_shape, face_shape), smem=1, args=(block_pos, features, cotangent)
    )
    flip_one, flip_two = flipped(weight_one), flipped(weight_two)
    halo = exchange(grid, lo, hi)
    term = jax.ShapeDtypeStruct((27 * C, C), BF)
    fields, lo, hi, term_one, term_two = call(
        lambda *refs: middle_kernel(scale, *refs),
        (fields_shape, face_shape, face_shape, term, term),
        scratch=(pad, pad, shifts, pltpu.VMEM((ROWS, C), F32)),
        args=(grid, *halo, weight_one, flip_two),
    )
    grad_one, grad_two = reduce_terms(jnp.concatenate([term_one, term_two], axis=0))
    halo = exchange(fields, lo, hi)
    output, input_grad = call(
        final_kernel,
        (jax.ShapeDtypeStruct(features.shape, BF), jax.ShapeDtypeStruct(features.shape, F32)),
        scratch=(pad, shifts),
        smem=1,
        args=(block_pos, grid, fields, *halo, weight_two, flip_one),
    )
    return output, input_grad, grad_one, grad_two


def solution(mesh):
    split = Mesh(mesh.devices.reshape(DIMS), NAMES)
    rows = P(NAMES, None)
    return jax.shard_map(
        per_device,
        mesh=split,
        in_specs=(rows, rows, P(NAMES), P(), P()),
        out_specs=(rows, rows, P(), P()),
        check_vma=False,
    )
```

```python
import jax
import jax.numpy as jnp
from jax import lax
from jax.experimental import pallas as pl
from jax.experimental.pallas import tpu as pltpu
from jax.sharding import Mesh
from jax.sharding import PartitionSpec as P

LBY, LBZ = 2, 3
SLOTS = 8
C = 128
GX, GY, GZ = 8, 8, 16
PX, PY = GX + 2, GY + 2
ROWS = GX * GY * GZ
PAD_ROWS = PX * PY * GZ
DIMS = (2, 4, 4, 4, 2, 2)
NAMES = ("y_lo", "x", "z_hi", "z_lo", "y_hi", "core")
INTERPRET = False
BF = jnp.bfloat16
F32 = jnp.float32


def grid_row(pos_ref, index):
    slot = index >> 6
    pos = jnp.full(index.shape, -1, jnp.int32)
    for s in range(SLOTS):
        pos = jnp.where(slot == s, pos_ref[s], pos)
    safe = jnp.maximum(pos, 0)
    bx = (safe >= 6).astype(jnp.int32)
    rest = safe - 6 * bx
    by = (rest >= 3).astype(jnp.int32)
    bz = rest - 3 * by
    vx = (index >> 4) & 3
    vy = (index >> 2) & 3
    vz = index & 3
    row = ((bx * 4 + vx) * GY + by * 4 + vy) * GZ + bz * 4 + vz
    return jnp.where(pos >= 0, row, -1)


def dot(a, b, dims=((1,), (0,))):
    return lax.dot_general(a, b, (dims, ((), ())), preferred_element_type=F32)


def place_kernel(pos_ref, feat_ref, cot_ref, grid_ref, lo_ref, hi_ref):
    target = grid_row(pos_ref, lax.broadcasted_iota(jnp.int32, (1, SLOTS * 64), 1))
    rows = lax.broadcasted_iota(jnp.int32, (ROWS, SLOTS * 64), 0)
    perm = (rows == target).astype(F32).astype(BF)
    for field, ref in enumerate((feat_ref, cot_ref)):
        placed = dot(perm, ref[...]).astype(BF)
        grid_ref[field] = placed
        lo_ref[field] = placed[: GY * GZ]
        hi_ref[field] = placed[ROWS - GY * GZ :]
    grid_ref[2] = dot(perm, jnp.ones((SLOTS * 64, C), BF)).astype(BF)


def z_shifts(field, flip=False):
    rows = field.shape[0]
    wide = field.astype(F32)
    before = pltpu.roll(wide, 1, 0).astype(BF)
    after = pltpu.roll(wide, rows - 1, 0).astype(BF)
    return jnp.concatenate([after, field, before] if flip else [before, field, after], axis=1)


def fill_pad(pad_ref, grid, x_lo, x_hi, y_lo, y_hi):
    pad_ref[1 : PX - 1, 1 : PY - 1] = grid.reshape(GX, GY, GZ, C)
    pad_ref[0, 1 : PY - 1] = x_lo.reshape(GY, GZ, C)
    pad_ref[PX - 1, 1 : PY - 1] = x_hi.reshape(GY, GZ, C)
    pad_ref[:, 0] = y_lo.reshape(PX, GZ, C)
    pad_ref[:, PY - 1] = y_hi.reshape(PX, GZ, C)


def conv(shift_ref, w_ref, flip):
    acc = None
    for k in range(9):
        dx, dy = divmod(k, 3)
        lhs = shift_ref[dx : dx + GX, dy : dy + GY].reshape(ROWS, 3 * C)
        at = 8 - k if flip else k
        term = dot(lhs, w_ref[at * 3 * C : (at + 1) * 3 * C, :])
        acc = term if acc is None else acc + term
    return acc


def middle_kernel(
    scale, grid_ref, xlo_ref, xhi_ref, ylo_ref, yhi_ref, w1_ref, w2f_ref,
    fields_ref, lo_ref, hi_ref, terms_ref, padx_ref, padu_ref, shift_ref, pre_ref,
):
    mask = grid_ref[2].astype(F32)
    fill_pad(padx_ref, grid_ref[0], xlo_ref[0], xhi_ref[0], ylo_ref[0], yhi_ref[0])
    fill_pad(padu_ref, grid_ref[1], xlo_ref[1], xhi_ref[1], ylo_ref[1], yhi_ref[1])
    shift_ref[...] = z_shifts(padx_ref[...].reshape(PAD_ROWS, C)).reshape(PX, PY, GZ, 3 * C)
    pre_ref[...] = conv(shift_ref, w1_ref, False)
    shift_ref[...] = z_shifts(padu_ref[...].reshape(PAD_ROWS, C), True).reshape(PX, PY, GZ, 3 * C)
    back = conv(shift_ref, w2f_ref, True)
    pre = pre_ref[...]
    sig = jax.nn.sigmoid(pre)
    hidden = (pre * sig * mask).astype(BF)
    hgrad = (back * (sig * (1.0 + pre * (1.0 - sig))) * mask).astype(BF)
    fields_ref[0] = hidden
    fields_ref[1] = hgrad
    for field, value in enumerate((hidden, hgrad)):
        lo_ref[field] = value[: GY * GZ]
        hi_ref[field] = value[ROWS - GY * GZ :]
    hz = z_shifts(hidden).T
    for k in range(9):
        dx, dy = divmod(k, 3)
        rhs = padu_ref[2 - dx : 2 - dx + GX, 2 - dy : 2 - dy + GY].reshape(ROWS, C)
        terms_ref[(27 + 3 * k) * C : (30 + 3 * k) * C, :] = (dot(hz, rhs) * scale).astype(BF)
    gz = z_shifts(hgrad).T
    for k in range(9):
        dx, dy = divmod(k, 3)
        rhs = padx_ref[dx : dx + GX, dy : dy + GY].reshape(ROWS, C)
        prod = dot(gz, rhs) * scale
        for oz in range(3):
            block = prod[(2 - oz) * C : (3 - oz) * C, :].T
            terms_ref[(3 * k + oz) * C : (3 * k + oz + 1) * C, :] = block.astype(BF)


def final_kernel(
    pos_ref, grid_ref, fields_ref, xlo_ref, xhi_ref, ylo_ref, yhi_ref, w2_ref, w1f_ref,
    out_ref, grad_ref, pad_ref, shift_ref,
):
    target = grid_row(pos_ref, lax.broadcasted_iota(jnp.int32, (SLOTS * 64, 1), 0))
    rows = lax.broadcasted_iota(jnp.int32, (SLOTS * 64, ROWS), 1)
    perm = (rows == target).astype(F32).astype(BF)
    for field, w_ref in enumerate((w2_ref, w1f_ref)):
        fill_pad(pad_ref, fields_ref[field], xlo_ref[field], xhi_ref[field], ylo_ref[field], yhi_ref[field])
        shift_ref[...] = z_shifts(pad_ref[...].reshape(PAD_ROWS, C), field == 1).reshape(PX, PY, GZ, 3 * C)
        value = conv(shift_ref, w_ref, field == 1) + grid_ref[field].astype(F32)
        high = value.astype(BF)
        if field == 0:
            out_ref[...] = dot(perm, high).astype(BF)
        else:
            low = (value - high.astype(F32)).astype(BF)
            grad_ref[...] = dot(perm, high) + dot(perm, low)


def call(kernel, outs, scratch=(), smem=0, args=()):
    specs = [pl.BlockSpec(memory_space=pltpu.SMEM)] * smem
    specs += [pl.BlockSpec(memory_space=pltpu.VMEM)] * (len(args) - smem)
    return pl.pallas_call(
        kernel,
        out_shape=outs,
        in_specs=specs,
        out_specs=jax.tree.map(lambda _: pl.BlockSpec(memory_space=pltpu.VMEM), outs),
        scratch_shapes=list(scratch),
        compiler_params=pltpu.CompilerParams(vmem_limit_bytes=56 << 20),
        interpret=INTERPRET,
    )(*args)


def transposed(weight):
    return weight.reshape(27, C, C).transpose(0, 2, 1).reshape(27 * C, C)


def ring(axes):
    count = lax.axis_size(axes)
    forward = [(i, i + 1) for i in range(count - 1)]
    return forward, [(b, a) for a, b in forward]


GXN = ("y_lo", "x", "z_hi", "z_lo")
GYN = ("y_hi", "core")
YX = ("y_hi", "y_lo", "x")


def exchange(fields, lo, hi):
    forward, backward = ring(GXN)
    x_lo = lax.ppermute(hi, GXN, forward)
    x_hi = lax.ppermute(lo, GXN, backward)
    grid = fields.reshape(-1, GX, GY, GZ, C)[:2]
    lows = x_lo.reshape(2, 1, GY, GZ, C)
    highs = x_hi.reshape(2, 1, GY, GZ, C)

    def face(y):
        return jnp.concatenate([lows[:, :, y], grid[:, :, y], highs[:, :, y]], axis=1).reshape(2, PX * GZ, C)

    forward, backward = ring(GYN)
    y_lo = lax.ppermute(face(GY - 1), GYN, forward)
    y_hi = lax.ppermute(face(0), GYN, backward)
    return x_lo, x_hi, y_lo, y_hi


def swap(values, axes):
    return lax.all_to_all(values, axes, 0, 0, tiled=True)


def scatter_sum(values, axes):
    count = lax.axis_size(axes)
    return swap(values.reshape(count, -1, C), axes).astype(F32).sum(axis=0)


def gather(values, axes):
    return swap(jnp.broadcast_to(values, (lax.axis_size(axes), *values.shape)), axes)


def reduce_terms(terms):
    share = scatter_sum(terms, "core").astype(BF)
    share = scatter_sum(share, YX)
    rows = share.shape[0]
    padded = -(-rows // (8 * lax.axis_size("z_lo"))) * 8 * lax.axis_size("z_lo")
    share = jnp.pad(share, ((0, padded - rows), (0, 0)))
    share = scatter_sum(share, "z_lo")
    share = gather(share, "z_hi").sum(axis=0).astype(BF)
    share = gather(share, "z_lo").reshape(padded, C)[:rows]
    share = gather(share, YX).reshape(-1, C)
    other = lax.ppermute(share, "core", [(0, 1), (1, 0)])
    first = lax.axis_index("core") == 0
    return jnp.where(first, share, other).astype(F32), jnp.where(first, other, share).astype(F32)


def per_device(features, cotangent, block_pos, weight_one, weight_two):
    total_rows = block_pos.shape[0] * 64 * lax.axis_size(NAMES)
    scale = float(total_rows) ** -0.5
    grid_shape = jax.ShapeDtypeStruct((3, ROWS, C), BF)
    face_shape = jax.ShapeDtypeStruct((2, GY * GZ, C), BF)
    fields_shape = jax.ShapeDtypeStruct((2, ROWS, C), BF)
    pad = pltpu.VMEM((PX, PY, GZ, C), BF)
    shifts = pltpu.VMEM((PX, PY, GZ, 3 * C), BF)
    grid, lo, hi = call(
        place_kernel, (grid_shape, face_shape, face_shape), smem=1, args=(block_pos, features, cotangent)
    )
    flip_one, flip_two = transposed(weight_one), transposed(weight_two)
    halo = exchange(grid, lo, hi)
    terms_shape = jax.ShapeDtypeStruct((54 * C, C), BF)
    fields, lo, hi, terms = call(
        lambda *refs: middle_kernel(scale, *refs),
        (fields_shape, face_shape, face_shape, terms_shape),
        scratch=(pad, pad, shifts, pltpu.VMEM((ROWS, C), F32)),
        args=(grid, *halo, weight_one, flip_two),
    )
    grad_one, grad_two = reduce_terms(terms)
    halo = exchange(fields, lo, hi)
    output, input_grad = call(
        final_kernel,
        (jax.ShapeDtypeStruct(features.shape, BF), jax.ShapeDtypeStruct(features.shape, F32)),
        scratch=(pad, shifts),
        smem=1,
        args=(block_pos, grid, fields, *halo, weight_two, flip_one),
    )
    return output, input_grad, grad_one, grad_two


def solution(mesh):
    split = Mesh(mesh.devices.reshape(DIMS), NAMES)
    rows = P(NAMES, None)
    return jax.shard_map(
        per_device,
        mesh=split,
        in_specs=(rows, rows, P(NAMES), P(), P()),
        out_specs=(rows, rows, P(), P()),
        check_vma=False,
    )
```

```python
import jax
import jax.numpy as jnp
from jax import lax
from jax.experimental import pallas as pl
from jax.experimental.pallas import tpu as pltpu
from jax.sharding import Mesh
from jax.sharding import PartitionSpec as P

LBY, LBZ = 2, 3
SLOTS = 8
C = 128
GX, GY, GZ = 8, 8, 16
EX, EY = GX + 2, GY + 2
PX, PY = GX + 4, GY + 4
ROWS = GX * GY * GZ
EXT_ROWS = EX * EY * GZ
PAD_ROWS = PX * PY * GZ
FACE = 2 * GY * GZ
DIMS = (2, 4, 4, 4, 2, 2)
NAMES = ("y_lo", "x", "z_hi", "z_lo", "y_hi", "core")
INTERPRET = False
BF = jnp.bfloat16
F32 = jnp.float32


def grid_row(pos_ref, index):
    slot = index >> 6
    pos = jnp.full(index.shape, -1, jnp.int32)
    for s in range(SLOTS):
        pos = jnp.where(slot == s, pos_ref[s], pos)
    safe = jnp.maximum(pos, 0)
    bx = (safe >= 6).astype(jnp.int32)
    rest = safe - 6 * bx
    by = (rest >= 3).astype(jnp.int32)
    bz = rest - 3 * by
    vx = (index >> 4) & 3
    vy = (index >> 2) & 3
    vz = index & 3
    row = ((bx * 4 + vx) * GY + by * 4 + vy) * GZ + bz * 4 + vz
    return jnp.where(pos >= 0, row, -1)


def dot(a, b, dims=((1,), (0,))):
    return lax.dot_general(a, b, (dims, ((), ())), preferred_element_type=F32)


def place_kernel(pos_ref, feat_ref, cot_ref, grid_ref, xlo_ref, xhi_ref, ylo_ref, yhi_ref):
    target = grid_row(pos_ref, lax.broadcasted_iota(jnp.int32, (1, SLOTS * 64), 1))
    rows = lax.broadcasted_iota(jnp.int32, (ROWS, SLOTS * 64), 0)
    perm = (rows == target).astype(F32).astype(BF)
    mask = dot(perm, jnp.ones((SLOTS * 64, C), BF))
    z = lax.broadcasted_iota(jnp.int32, (ROWS, C), 0) & (GZ - 1)
    flags = jnp.where(z == 13, pltpu.roll(mask, 13, 0) + 2.0 * pltpu.roll(mask, 5, 0), 0.0)
    flags = jnp.where(z == 14, pltpu.roll(mask, 10, 0), flags)
    for field, ref in enumerate((feat_ref, cot_ref)):
        placed = dot(perm, ref[...])
        placed = (placed + flags if field == 0 else placed).astype(BF)
        grid_ref[field] = placed
        xlo_ref[field] = placed[:FACE]
        xhi_ref[field] = placed[ROWS - FACE :]
        columns = placed.reshape(GX, GY * GZ, C)
        ylo_ref[field] = columns[:, : 2 * GZ]
        yhi_ref[field] = columns[:, (GY - 2) * GZ :]


def z_shifts(field, flip=False):
    rows = field.shape[0]
    wide = field.astype(F32)
    before = pltpu.roll(wide, 1, 0).astype(BF)
    after = pltpu.roll(wide, rows - 1, 0).astype(BF)
    return jnp.concatenate([after, field, before] if flip else [before, field, after], axis=1)


def fill_pad(pad_ref, grid, x_lo, x_hi, y_lo, y_hi):
    pad_ref[2 : PX - 2, 2 : PY - 2] = grid.reshape(GX, GY, GZ, C)
    pad_ref[:2, 2 : PY - 2] = x_lo.reshape(2, GY, GZ, C)
    pad_ref[PX - 2 :, 2 : PY - 2] = x_hi.reshape(2, GY, GZ, C)
    pad_ref[:, :2] = y_lo.reshape(PX, 2, GZ, C)
    pad_ref[:, PY - 2 :] = y_hi.reshape(PX, 2, GZ, C)


def conv(shift_ref, w_ref, flip):
    nx, ny = shift_ref.shape[0] - 2, shift_ref.shape[1] - 2
    acc = None
    for k in range(9):
        dx, dy = divmod(k, 3)
        lhs = shift_ref[dx : dx + nx, dy : dy + ny].reshape(nx * ny * GZ, 3 * C)
        at = 8 - k if flip else k
        term = dot(lhs, w_ref[at * 3 * C : (at + 1) * 3 * C, :])
        acc = term if acc is None else acc + term
    return acc


def active_rows(field):
    both, middle = field[:, :, 13:14], field[:, :, 14:15]
    high = (both > 1.5).astype(F32)
    low = both - 2.0 * high
    z = lax.broadcasted_iota(jnp.int32, field.shape, 2)
    upper = jnp.where(z < 8, jnp.broadcast_to(middle, field.shape), jnp.broadcast_to(high, field.shape))
    mask = jnp.where(z < 4, jnp.broadcast_to(low, field.shape), upper)
    return jnp.where(z < 12, mask, 0.0)


def middle_kernel(
    scale, grid_ref, xlo_ref, xhi_ref, ylo_ref, yhi_ref, w1_ref, w2t_ref,
    fields_ref, terms_ref, padx_ref, padu_ref, shift_ref, pre_ref,
):
    fill_pad(padx_ref, grid_ref[0], xlo_ref[0], xhi_ref[0], ylo_ref[0], yhi_ref[0])
    fill_pad(padu_ref, grid_ref[1], xlo_ref[1], xhi_ref[1], ylo_ref[1], yhi_ref[1])
    shift_ref[...] = z_shifts(padx_ref[...].reshape(PAD_ROWS, C)).reshape(PX, PY, GZ, 3 * C)
    pre_ref[...] = conv(shift_ref, w1_ref, False)
    shift_ref[...] = z_shifts(padu_ref[...].reshape(PAD_ROWS, C), True).reshape(PX, PY, GZ, 3 * C)
    back = conv(shift_ref, w2t_ref, True)
    pre = pre_ref[...]
    mask = active_rows(padx_ref[1 : PX - 1, 1 : PY - 1].astype(F32)).reshape(EXT_ROWS, C)
    sig = jax.nn.sigmoid(pre)
    fields_ref[0] = (pre * sig * mask).astype(BF).reshape(EX, EY, GZ, C)
    fields_ref[1] = (back * (sig * (1.0 + pre * (1.0 - sig))) * mask).astype(BF).reshape(EX, EY, GZ, C)

    def own(field):
        return fields_ref[field, 1 : EX - 1, 1 : EY - 1].reshape(ROWS, C)

    hz = z_shifts(own(0)).T
    for k in range(9):
        dx, dy = divmod(k, 3)
        rhs = padu_ref[3 - dx : 3 - dx + GX, 3 - dy : 3 - dy + GY].reshape(ROWS, C)
        terms_ref[(27 + 3 * k) * C : (30 + 3 * k) * C, :] = (dot(hz, rhs) * scale).astype(BF)
    gz = z_shifts(own(1)).T
    for k in range(9):
        dx, dy = divmod(k, 3)
        rhs = padx_ref[dx + 1 : dx + 1 + GX, dy + 1 : dy + 1 + GY].reshape(ROWS, C)
        prod = dot(gz, rhs) * scale
        for oz in range(3):
            block = prod[(2 - oz) * C : (3 - oz) * C, :].T
            terms_ref[(3 * k + oz) * C : (3 * k + oz + 1) * C, :] = block.astype(BF)


def final_kernel(pos_ref, grid_ref, fields_ref, w2_ref, w1t_ref, out_ref, grad_ref, shift_ref):
    target = grid_row(pos_ref, lax.broadcasted_iota(jnp.int32, (SLOTS * 64, 1), 0))
    rows = lax.broadcasted_iota(jnp.int32, (SLOTS * 64, ROWS), 1)
    perm = (rows == target).astype(F32).astype(BF)
    for field, w_ref in enumerate((w2_ref, w1t_ref)):
        shift_ref[...] = z_shifts(fields_ref[field].reshape(EXT_ROWS, C), field == 1).reshape(EX, EY, GZ, 3 * C)
        value = conv(shift_ref, w_ref, field == 1) + grid_ref[field].astype(F32)
        high = value.astype(BF)
        if field == 0:
            out_ref[...] = dot(perm, high).astype(BF)
        else:
            low = (value - high.astype(F32)).astype(BF)
            grad_ref[...] = dot(perm, high) + dot(perm, low)


def call(kernel, outs, scratch=(), smem=0, args=(), cost=None):
    specs = [pl.BlockSpec(memory_space=pltpu.SMEM)] * smem
    specs += [pl.BlockSpec(memory_space=pltpu.VMEM)] * (len(args) - smem)
    return pl.pallas_call(
        kernel,
        out_shape=outs,
        in_specs=specs,
        out_specs=jax.tree.map(lambda _: pl.BlockSpec(memory_space=pltpu.VMEM), outs),
        scratch_shapes=list(scratch),
        compiler_params=pltpu.CompilerParams(vmem_limit_bytes=56 << 20),
        interpret=INTERPRET,
        cost_estimate=cost,
    )(*args)


def transposed(weight):
    return weight.reshape(27, C, C).transpose(0, 2, 1).reshape(27 * C, C)


def ring(axes):
    count = lax.axis_size(axes)
    forward = [(i, i + 1) for i in range(count - 1)]
    return forward, [(b, a) for a, b in forward]


GXN = ("y_lo", "x", "z_hi", "z_lo")
GYN = ("y_hi", "core")
YX = ("y_hi", "y_lo", "x")


def exchange(x_faces, y_faces):
    forward, backward = ring(GXN)
    x_lo = lax.ppermute(x_faces[1], GXN, forward)
    x_hi = lax.ppermute(x_faces[0], GXN, backward)

    def face(y):
        at = (GY - 2) * GZ if y else 0
        ends = [end.reshape(2, 2, GY * GZ, C)[:, :, at : at + 2 * GZ] for end in (x_lo, x_hi)]
        return jnp.concatenate([ends[0], y_faces[y], ends[1]], axis=1)

    forward, backward = ring(GYN)
    y_lo = lax.ppermute(face(1), GYN, forward)
    y_hi = lax.ppermute(face(0), GYN, backward)
    return x_lo, x_hi, y_lo, y_hi


def swap(values, axes):
    return lax.all_to_all(values, axes, 0, 0, tiled=True)


def scatter_sum(values, axes):
    count = lax.axis_size(axes)
    return swap(values.reshape(count, -1, C), axes).astype(F32).sum(axis=0)


def gather(values, axes):
    return swap(jnp.broadcast_to(values, (lax.axis_size(axes), *values.shape)), axes)


def reduce_terms(terms):
    share = scatter_sum(terms, "core").astype(BF)
    share = scatter_sum(share, YX)
    rows = share.shape[0]
    padded = -(-rows // (8 * lax.axis_size("z_lo"))) * 8 * lax.axis_size("z_lo")
    share = jnp.pad(share, ((0, padded - rows), (0, 0)))
    share = scatter_sum(share, "z_lo")
    share = gather(share, "z_hi").sum(axis=0).astype(BF)
    share = gather(share, "z_lo").reshape(padded, C)[:rows]
    share = gather(share, YX).reshape(-1, C)
    other = lax.ppermute(share, "core", [(0, 1), (1, 0)])
    first = lax.axis_index("core") == 0
    return jnp.where(first, share, other).astype(F32), jnp.where(first, other, share).astype(F32)


def per_device(features, cotangent, block_pos, weight_one, weight_two):
    total_rows = block_pos.shape[0] * 64 * lax.axis_size(NAMES)
    scale = float(total_rows) ** -0.5
    face_x = jax.ShapeDtypeStruct((2, FACE, C), BF)
    face_y = jax.ShapeDtypeStruct((2, GX, 2 * GZ, C), BF)
    grid, *faces = call(
        place_kernel,
        (jax.ShapeDtypeStruct((2, ROWS, C), BF), face_x, face_x, face_y, face_y),
        smem=1,
        args=(block_pos, features, cotangent),
    )
    halo = exchange(faces[:2], faces[2:])
    pad = pltpu.VMEM((PX, PY, GZ, C), BF)
    fields, terms = call(
        lambda *refs: middle_kernel(scale, *refs),
        (jax.ShapeDtypeStruct((2, EX, EY, GZ, C), BF), jax.ShapeDtypeStruct((54 * C, C), BF)),
        scratch=(pad, pad, pltpu.VMEM((PX, PY, GZ, 3 * C), BF), pltpu.VMEM((EXT_ROWS, C), F32)),
        args=(grid, *halo, weight_one, transposed(weight_two)),
    )
    output, input_grad = call(
        final_kernel,
        (jax.ShapeDtypeStruct(features.shape, BF), jax.ShapeDtypeStruct(features.shape, F32)),
        scratch=(pltpu.VMEM((EX, EY, GZ, 3 * C), BF),),
        smem=1,
        args=(block_pos, grid, fields, weight_two, transposed(weight_one)),
        cost=pl.CostEstimate(flops=2 * 2 * 27 * ROWS * C * C, transcendentals=0, bytes_accessed=24 << 20),
    )
    grad_one, grad_two = reduce_terms(terms)
    return output, input_grad, grad_one, grad_two


def solution(mesh):
    split = Mesh(mesh.devices.reshape(DIMS), NAMES)
    rows = P(NAMES, None)
    return jax.shard_map(
        per_device,
        mesh=split,
        in_specs=(rows, rows, P(NAMES), P(), P()),
        out_specs=(rows, rows, P(), P()),
        check_vma=False,
    )
```

```python
import jax
import jax.numpy as jnp
from jax import lax
from jax.experimental import pallas as pl
from jax.experimental.pallas import tpu as pltpu
from jax.sharding import Mesh
from jax.sharding import PartitionSpec as P


SLOTS = 8
C = 128
GX, GY, GZ = 8, 8, 16
EX, EY = GX + 2, GY + 2
PX, PY = GX + 4, GY + 4
ROWS = GX * GY * GZ
EXT_ROWS = EX * EY * GZ
PAD_ROWS = PX * PY * GZ
FACE = 2 * GY * GZ
DIMS = (2, 4, 4, 4, 2, 2)
NAMES = ("y_lo", "x", "z_hi", "z_lo", "y_hi", "core")
INTERPRET = False
BF = jnp.bfloat16
F32 = jnp.float32


def grid_row(pos_ref, index):
    slot = index >> 6
    pos = jnp.full(index.shape, -1, jnp.int32)
    for s in range(SLOTS):
        pos = jnp.where(slot == s, pos_ref[s], pos)
    safe = jnp.maximum(pos, 0)
    bx = (safe >= 6).astype(jnp.int32)
    rest = safe - 6 * bx
    by = (rest >= 3).astype(jnp.int32)
    bz = rest - 3 * by
    vx = (index >> 4) & 3
    vy = (index >> 2) & 3
    vz = index & 3
    row = ((bx * 4 + vx) * GY + by * 4 + vy) * GZ + bz * 4 + vz
    return jnp.where(pos >= 0, row, -1)


def dot(a, b, dims=((1,), (0,))):
    return lax.dot_general(a, b, (dims, ((), ())), preferred_element_type=F32)


def place_kernel(pos_ref, feat_ref, cot_ref, grid_ref, xlo_ref, xhi_ref, ylo_ref, yhi_ref):
    target = grid_row(pos_ref, lax.broadcasted_iota(jnp.int32, (1, SLOTS * 64), 1))
    rows = lax.broadcasted_iota(jnp.int32, (ROWS, SLOTS * 64), 0)
    perm = (rows == target).astype(F32).astype(BF)
    mask = dot(perm, jnp.ones((SLOTS * 64, C), BF))
    z = lax.broadcasted_iota(jnp.int32, (ROWS, C), 0) & (GZ - 1)
    flags = jnp.where(z == 13, pltpu.roll(mask, 13, 0) + 2.0 * pltpu.roll(mask, 5, 0), 0.0)
    flags = jnp.where(z == 14, pltpu.roll(mask, 10, 0), flags)
    for field, ref in enumerate((feat_ref, cot_ref)):
        placed = dot(perm, ref[...])
        placed = (placed + flags if field == 0 else placed).astype(BF)
        grid_ref[field] = placed
        xlo_ref[field] = placed[:FACE]
        xhi_ref[field] = placed[ROWS - FACE :]
        columns = placed.reshape(GX, GY * GZ, C)
        ylo_ref[field] = columns[:, : 2 * GZ]
        yhi_ref[field] = columns[:, (GY - 2) * GZ :]


def z_shifts(field, flip=False):
    rows = field.shape[0]
    wide = field.astype(F32)
    before = pltpu.roll(wide, 1, 0).astype(BF)
    after = pltpu.roll(wide, rows - 1, 0).astype(BF)
    return jnp.concatenate([after, field, before] if flip else [before, field, after], axis=1)


def fill_pad(pad_ref, grid, x_lo, x_hi, y_lo, y_hi):
    pad_ref[2 : PX - 2, 2 : PY - 2] = grid.reshape(GX, GY, GZ, C)
    pad_ref[:2, 2 : PY - 2] = x_lo.reshape(2, GY, GZ, C)
    pad_ref[PX - 2 :, 2 : PY - 2] = x_hi.reshape(2, GY, GZ, C)
    pad_ref[:, :2] = y_lo.reshape(PX, 2, GZ, C)
    pad_ref[:, PY - 2 :] = y_hi.reshape(PX, 2, GZ, C)


def conv(shift_ref, w_ref, flip):
    nx, ny = shift_ref.shape[0] - 2, shift_ref.shape[1] - 2

    def weight(dx, dy):
        k = 3 * dx + dy
        at = 8 - k if flip else k
        return w_ref[at * 3 * C : (at + 1) * 3 * C, :]

    def product(x, y, mx, my, rhs):
        lhs = shift_ref[x : x + mx, y : y + my].reshape(mx * my * GZ, 3 * C)
        return dot(lhs, rhs).reshape(mx, my, GZ, rhs.shape[1])

    acc = product(2, 2, nx, ny, weight(2, 2))
    for dx in range(3):
        pair = product(dx, 0, nx, ny + 1, jnp.concatenate([weight(dx, 0), weight(dx, 1)], axis=1))
        acc = acc + pair[:, :ny, :, :C] + pair[:, 1:, :, C:]
    pair = product(0, 2, nx + 1, ny, jnp.concatenate([weight(0, 2), weight(1, 2)], axis=1))
    return acc + pair[:nx, :, :, :C] + pair[1:, :, :, C:]


def active_rows(field):
    both, middle = field[:, :, 13:14], field[:, :, 14:15]
    high = (both > 1.5).astype(F32)
    low = both - 2.0 * high
    z = lax.broadcasted_iota(jnp.int32, field.shape, 2)
    upper = jnp.where(z < 8, jnp.broadcast_to(middle, field.shape), jnp.broadcast_to(high, field.shape))
    mask = jnp.where(z < 4, jnp.broadcast_to(low, field.shape), upper)
    return jnp.where(z < 12, mask, 0.0)


def middle_kernel(
    scale, grid_ref, xlo_ref, xhi_ref, ylo_ref, yhi_ref, w1_ref, w2t_ref,
    fields_ref, terms_ref, padx_ref, padu_ref, shift_ref, pre_ref,
):
    fill_pad(padx_ref, grid_ref[0], xlo_ref[0], xhi_ref[0], ylo_ref[0], yhi_ref[0])
    fill_pad(padu_ref, grid_ref[1], xlo_ref[1], xhi_ref[1], ylo_ref[1], yhi_ref[1])
    shift_ref[...] = z_shifts(padx_ref[...].reshape(PAD_ROWS, C)).reshape(PX, PY, GZ, 3 * C)
    pre_ref[...] = conv(shift_ref, w1_ref, False).reshape(EXT_ROWS, C)
    shift_ref[...] = z_shifts(padu_ref[...].reshape(PAD_ROWS, C), True).reshape(PX, PY, GZ, 3 * C)
    back = conv(shift_ref, w2t_ref, True).reshape(EXT_ROWS, C)
    pre = pre_ref[...]
    mask = active_rows(padx_ref[1 : PX - 1, 1 : PY - 1].astype(F32)).reshape(EXT_ROWS, C)
    sig = jax.nn.sigmoid(pre)
    fields_ref[0] = (pre * sig * mask).astype(BF).reshape(EX, EY, GZ, C)
    fields_ref[1] = (back * (sig * (1.0 + pre * (1.0 - sig))) * mask).astype(BF).reshape(EX, EY, GZ, C)

    def own(field):
        return fields_ref[field, 1 : EX - 1, 1 : EY - 1].reshape(ROWS, C)

    def products(lhs, rhs_of):
        for first in range(0, 9, 2):
            ks = range(first, min(first + 2, 9))
            prod = dot(lhs, jnp.concatenate([rhs_of(*divmod(k, 3)).reshape(ROWS, C) for k in ks], axis=1)) * scale
            for n, k in enumerate(ks):
                yield k, prod[:, n * C : (n + 1) * C]

    hz = z_shifts(own(0)).T
    for k, prod in products(hz, lambda dx, dy: padu_ref[3 - dx : 3 - dx + GX, 3 - dy : 3 - dy + GY]):
        terms_ref[(27 + 3 * k) * C : (30 + 3 * k) * C, :] = prod.astype(BF)
    gz = z_shifts(own(1)).T
    for k, prod in products(gz, lambda dx, dy: padx_ref[dx + 1 : dx + 1 + GX, dy + 1 : dy + 1 + GY]):
        for oz in range(3):
            block = prod[(2 - oz) * C : (3 - oz) * C, :].T
            terms_ref[(3 * k + oz) * C : (3 * k + oz + 1) * C, :] = block.astype(BF)


def final_kernel(pos_ref, grid_ref, fields_ref, w2_ref, w1t_ref, out_ref, grad_ref, shift_ref):
    target = grid_row(pos_ref, lax.broadcasted_iota(jnp.int32, (SLOTS * 64, 1), 0))
    rows = lax.broadcasted_iota(jnp.int32, (SLOTS * 64, ROWS), 1)
    perm = (rows == target).astype(F32).astype(BF)
    for field, w_ref in enumerate((w2_ref, w1t_ref)):
        shift_ref[...] = z_shifts(fields_ref[field].reshape(EXT_ROWS, C), field == 1).reshape(EX, EY, GZ, 3 * C)
        value = conv(shift_ref, w_ref, field == 1).reshape(ROWS, C) + grid_ref[field].astype(F32)
        high = value.astype(BF)
        if field == 0:
            out_ref[...] = dot(perm, high).astype(BF)
        else:
            low = (value - high.astype(F32)).astype(BF)
            grad_ref[...] = dot(perm, high) + dot(perm, low)


def call(kernel, outs, scratch=(), smem=0, args=(), cost=None):
    specs = [pl.BlockSpec(memory_space=pltpu.SMEM)] * smem
    specs += [pl.BlockSpec(memory_space=pltpu.VMEM)] * (len(args) - smem)
    return pl.pallas_call(
        kernel,
        out_shape=outs,
        in_specs=specs,
        out_specs=jax.tree.map(lambda _: pl.BlockSpec(memory_space=pltpu.VMEM), outs),
        scratch_shapes=list(scratch),
        compiler_params=pltpu.CompilerParams(vmem_limit_bytes=56 << 20),
        interpret=INTERPRET,
        cost_estimate=cost,
    )(*args)


def transposed(weight):
    return weight.reshape(27, C, C).transpose(0, 2, 1).reshape(27 * C, C)


def ring(axes):
    count = lax.axis_size(axes)
    forward = [(i, i + 1) for i in range(count - 1)]
    return forward, [(b, a) for a, b in forward]


GXN = ("y_lo", "x", "z_hi", "z_lo")
GYN = ("y_hi", "core")
YX = ("y_hi", "y_lo", "x")


def exchange(x_faces, y_faces):
    forward, backward = ring(GXN)
    x_lo = lax.ppermute(x_faces[1], GXN, forward)
    x_hi = lax.ppermute(x_faces[0], GXN, backward)

    def face(y):
        at = (GY - 2) * GZ if y else 0
        ends = [end.reshape(2, 2, GY * GZ, C)[:, :, at : at + 2 * GZ] for end in (x_lo, x_hi)]
        return jnp.concatenate([ends[0], y_faces[y], ends[1]], axis=1)

    forward, backward = ring(GYN)
    y_lo = lax.ppermute(face(1), GYN, forward)
    y_hi = lax.ppermute(face(0), GYN, backward)
    return x_lo, x_hi, y_lo, y_hi


def swap(values, axes):
    return lax.all_to_all(values, axes, 0, 0, tiled=True)


def scatter_sum(values, axes):
    count = lax.axis_size(axes)
    return swap(values.reshape(count, -1, C), axes).astype(F32).sum(axis=0)


def gather(values, axes):
    return swap(jnp.broadcast_to(values, (lax.axis_size(axes), *values.shape)), axes)


def reduce_terms(terms):
    share = scatter_sum(terms, "core").astype(BF)
    share = scatter_sum(share, YX)
    rows = share.shape[0]
    padded = -(-rows // (8 * lax.axis_size("z_lo"))) * 8 * lax.axis_size("z_lo")
    share = jnp.pad(share, ((0, padded - rows), (0, 0)))
    share = scatter_sum(share, "z_lo")
    share = gather(share, "z_hi").sum(axis=0).astype(BF)
    share = gather(share, "z_lo").reshape(padded, C)[:rows]
    share = gather(share, YX).reshape(-1, C)
    other = lax.ppermute(share, "core", [(0, 1), (1, 0)])
    first = lax.axis_index("core") == 0
    return jnp.where(first, share, other).astype(F32), jnp.where(first, other, share).astype(F32)


def compute(features, cotangent, block_pos, weight_one, weight_two):
    total_rows = block_pos.shape[0] * 64 * lax.axis_size(NAMES)
    scale = float(total_rows) ** -0.5
    face_x = jax.ShapeDtypeStruct((2, FACE, C), BF)
    face_y = jax.ShapeDtypeStruct((2, GX, 2 * GZ, C), BF)
    grid, *faces = call(
        place_kernel,
        (jax.ShapeDtypeStruct((2, ROWS, C), BF), face_x, face_x, face_y, face_y),
        smem=1,
        args=(block_pos, features, cotangent),
    )
    halo = exchange(faces[:2], faces[2:])
    pad = pltpu.VMEM((PX, PY, GZ, C), BF)
    fields, terms = call(
        lambda *refs: middle_kernel(scale, *refs),
        (jax.ShapeDtypeStruct((2, EX, EY, GZ, C), BF), jax.ShapeDtypeStruct((54 * C, C), BF)),
        scratch=(pad, pad, pltpu.VMEM((PX, PY, GZ, 3 * C), BF), pltpu.VMEM((EXT_ROWS, C), F32)),
        args=(grid, *halo, weight_one, transposed(weight_two)),
    )
    output, input_grad = call(
        final_kernel,
        (jax.ShapeDtypeStruct(features.shape, BF), jax.ShapeDtypeStruct(features.shape, F32)),
        scratch=(pltpu.VMEM((EX, EY, GZ, 3 * C), BF),),
        smem=1,
        args=(block_pos, grid, fields, weight_two, transposed(weight_one)),
        cost=pl.CostEstimate(flops=2 * 2 * 27 * ROWS * C * C, transcendentals=0, bytes_accessed=24 << 20),
    )
    grad_one, grad_two = reduce_terms(terms)
    return output, input_grad, grad_one, grad_two


def solution(mesh):
    split = Mesh(mesh.devices.reshape(DIMS), NAMES)
    rows = P(NAMES, None)
    return jax.shard_map(
        compute,
        mesh=split,
        in_specs=(rows, rows, P(NAMES), P(), P()),
        out_specs=(rows, rows, P(), P()),
        check_vma=False,
    )
```

```python
import jax
import jax.numpy as jnp
from jax import lax
from jax.experimental import pallas as pl
from jax.experimental.pallas import tpu as pltpu
from jax.sharding import Mesh
from jax.sharding import PartitionSpec as P


SLOTS = 8
C = 128
GX, GY, GZ = 8, 8, 16
EX, EY = GX + 2, GY + 2
PX, PY = GX + 4, GY + 4
ROWS = GX * GY * GZ
EXT_ROWS = EX * EY * GZ
PAD_ROWS = PX * PY * GZ
FACE = 2 * GY * GZ
DIMS = (2, 4, 4, 4, 2, 2)
NAMES = ("y_lo", "x", "z_hi", "z_lo", "y_hi", "core")
INTERPRET = False
BF = jnp.bfloat16
F32 = jnp.float32


def grid_row(pos_ref, index):
    slot = index >> 6
    pos = jnp.full(index.shape, -1, jnp.int32)
    for s in range(SLOTS):
        pos = jnp.where(slot == s, pos_ref[s], pos)
    safe = jnp.maximum(pos, 0)
    bx = (safe >= 6).astype(jnp.int32)
    rest = safe - 6 * bx
    by = (rest >= 3).astype(jnp.int32)
    bz = rest - 3 * by
    vx = (index >> 4) & 3
    vy = (index >> 2) & 3
    vz = index & 3
    row = ((bx * 4 + vx) * GY + by * 4 + vy) * GZ + bz * 4 + vz
    return jnp.where(pos >= 0, row, -1)


def dot(a, b, dims=((1,), (0,))):
    return lax.dot_general(a, b, (dims, ((), ())), preferred_element_type=F32)


def place_kernel(pos_ref, feat_ref, cot_ref, grid_ref, xlo_ref, xhi_ref, ylo_ref, yhi_ref):
    target = grid_row(pos_ref, lax.broadcasted_iota(jnp.int32, (1, SLOTS * 64), 1))
    rows = lax.broadcasted_iota(jnp.int32, (ROWS, SLOTS * 64), 0)
    perm = (rows == target).astype(F32).astype(BF)
    mask = dot(perm, jnp.ones((SLOTS * 64, C), BF))
    z = lax.broadcasted_iota(jnp.int32, (ROWS, C), 0) & (GZ - 1)
    flags = jnp.where(z == 13, pltpu.roll(mask, 13, 0) + 2.0 * pltpu.roll(mask, 5, 0), 0.0)
    flags = jnp.where(z == 14, pltpu.roll(mask, 10, 0), flags)
    for field, ref in enumerate((feat_ref, cot_ref)):
        placed = dot(perm, ref[...])
        placed = (placed + flags if field == 0 else placed).astype(BF)
        grid_ref[field] = placed
        xlo_ref[field] = placed[:FACE]
        xhi_ref[field] = placed[ROWS - FACE :]
        columns = placed.reshape(GX, GY * GZ, C)
        ylo_ref[field] = columns[:, : 2 * GZ]
        yhi_ref[field] = columns[:, (GY - 2) * GZ :]


def z_shifts(field, flip=False):
    rows = field.shape[0]
    wide = field.astype(F32)
    before = pltpu.roll(wide, 1, 0).astype(BF)
    after = pltpu.roll(wide, rows - 1, 0).astype(BF)
    return jnp.concatenate([after, field, before] if flip else [before, field, after], axis=1)


def fill_pad(pad_ref, grid, x_lo, x_hi, y_lo, y_hi):
    pad_ref[2 : PX - 2, 2 : PY - 2] = grid.reshape(GX, GY, GZ, C)
    pad_ref[:2, 2 : PY - 2] = x_lo.reshape(2, GY, GZ, C)
    pad_ref[PX - 2 :, 2 : PY - 2] = x_hi.reshape(2, GY, GZ, C)
    pad_ref[:, :2] = y_lo.reshape(PX, 2, GZ, C)
    pad_ref[:, PY - 2 :] = y_hi.reshape(PX, 2, GZ, C)


def conv(shift_ref, w_ref, flip):
    nx, ny = shift_ref.shape[0] - 2, shift_ref.shape[1] - 2

    def weight(dx, dy):
        k = 3 * dx + dy
        at = 8 - k if flip else k
        return w_ref[at * 3 * C : (at + 1) * 3 * C, :]

    def product(x, y, mx, my, rhs):
        lhs = shift_ref[x : x + mx, y : y + my].reshape(mx * my * GZ, 3 * C)
        return dot(lhs, rhs).reshape(mx, my, GZ, rhs.shape[1])

    acc = product(2, 2, nx, ny, weight(2, 2))
    for dx in range(3):
        pair = product(dx, 0, nx, ny + 1, jnp.concatenate([weight(dx, 0), weight(dx, 1)], axis=1))
        acc = acc + pair[:, :ny, :, :C] + pair[:, 1:, :, C:]
    pair = product(0, 2, nx + 1, ny, jnp.concatenate([weight(0, 2), weight(1, 2)], axis=1))
    return acc + pair[:nx, :, :, :C] + pair[1:, :, :, C:]


def active_rows(field):
    both, middle = field[:, :, 13:14], field[:, :, 14:15]
    high = (both > 1.5).astype(F32)
    low = both - 2.0 * high
    z = lax.broadcasted_iota(jnp.int32, field.shape, 2)
    upper = jnp.where(z < 8, jnp.broadcast_to(middle, field.shape), jnp.broadcast_to(high, field.shape))
    mask = jnp.where(z < 4, jnp.broadcast_to(low, field.shape), upper)
    return jnp.where(z < 12, mask, 0.0)


def middle_kernel(
    grid_ref, xlo_ref, xhi_ref, ylo_ref, yhi_ref, w1_ref, w2t_ref, pairs_ref, padx_ref, padu_ref, shift_ref, pre_ref,
):
    fill_pad(padx_ref, grid_ref[0], xlo_ref[0], xhi_ref[0], ylo_ref[0], yhi_ref[0])
    fill_pad(padu_ref, grid_ref[1], xlo_ref[1], xhi_ref[1], ylo_ref[1], yhi_ref[1])
    pairs_ref[0, 0] = padx_ref[1 : PX - 1, 1 : PY - 1]
    pairs_ref[1, 1] = padu_ref[1 : PX - 1, 1 : PY - 1]
    shift_ref[...] = z_shifts(padx_ref[...].reshape(PAD_ROWS, C)).reshape(PX, PY, GZ, 3 * C)
    pre_ref[...] = conv(shift_ref, w1_ref, False).reshape(EXT_ROWS, C)
    shift_ref[...] = z_shifts(padu_ref[...].reshape(PAD_ROWS, C), True).reshape(PX, PY, GZ, 3 * C)
    back = conv(shift_ref, w2t_ref, True).reshape(EXT_ROWS, C)
    pre = pre_ref[...]
    mask = active_rows(padx_ref[1 : PX - 1, 1 : PY - 1].astype(F32)).reshape(EXT_ROWS, C)
    sig = jax.nn.sigmoid(pre)
    pairs_ref[1, 0] = (pre * sig * mask).astype(BF).reshape(EX, EY, GZ, C)
    pairs_ref[0, 1] = (back * (sig * (1.0 + pre * (1.0 - sig))) * mask).astype(BF).reshape(EX, EY, GZ, C)


def gram_kernel(scale, which_ref, pair_ref, term_ref):
    del which_ref
    left = pair_ref[0, 0, 1 : EX - 1, 1 : EY - 1].reshape(ROWS, C)
    lhs = z_shifts(left).T
    for first in range(0, 9, 2):
        ks = range(first, min(first + 2, 9))
        starts = [(2 - k // 3, 2 - k % 3) for k in ks]
        rhs = [pair_ref[0, 1, x : x + GX, y : y + GY].reshape(ROWS, C) for x, y in starts]
        prod = dot(lhs, jnp.concatenate(rhs, axis=1)) * scale
        for n, k in enumerate(ks):
            term_ref[3 * k * C : 3 * (k + 1) * C, :] = prod[:, n * C : (n + 1) * C].astype(term_ref.dtype)


def gram(scale, which, pairs, dtype):
    spec = pltpu.PrefetchScalarGridSpec(
        num_scalar_prefetch=1,
        grid=(1,),
        in_specs=[pl.BlockSpec((1, 2, EX, EY, GZ, C), lambda i, which_ref: (which_ref[0], 0, 0, 0, 0, 0))],
        out_specs=pl.BlockSpec((27 * C, C), lambda i, which_ref: (0, 0)),
    )
    return pl.pallas_call(
        lambda *refs: gram_kernel(scale, *refs),
        grid_spec=spec,
        out_shape=jax.ShapeDtypeStruct((27 * C, C), dtype),
        compiler_params=pltpu.CompilerParams(vmem_limit_bytes=56 << 20),
        interpret=INTERPRET,
        cost_estimate=pl.CostEstimate(flops=2 * 27 * ROWS * C * C, transcendentals=0, bytes_accessed=9 << 20),
    )(which.reshape(1), pairs)


def final_kernel(pos_ref, pairs_ref, w2_ref, w1t_ref, out_ref, grad_ref, shift_ref):
    target = grid_row(pos_ref, lax.broadcasted_iota(jnp.int32, (SLOTS * 64, 1), 0))
    rows = lax.broadcasted_iota(jnp.int32, (SLOTS * 64, ROWS), 1)
    perm = (rows == target).astype(F32).astype(BF)
    for field, w_ref in enumerate((w2_ref, w1t_ref)):
        source = pairs_ref[1 - field, field].reshape(EXT_ROWS, C)
        shift_ref[...] = z_shifts(source, field == 1).reshape(EX, EY, GZ, 3 * C)
        straight = pairs_ref[field, field, 1 : EX - 1, 1 : EY - 1].reshape(ROWS, C)
        value = conv(shift_ref, w_ref, field == 1).reshape(ROWS, C) + straight.astype(F32)
        high = value.astype(BF)
        if field == 0:
            out_ref[...] = dot(perm, high).astype(BF)
        else:
            low = (value - high.astype(F32)).astype(BF)
            grad_ref[...] = dot(perm, high) + dot(perm, low)


def call(kernel, outs, scratch=(), smem=0, args=(), cost=None):
    specs = [pl.BlockSpec(memory_space=pltpu.SMEM)] * smem
    specs += [pl.BlockSpec(memory_space=pltpu.VMEM)] * (len(args) - smem)
    return pl.pallas_call(
        kernel,
        out_shape=outs,
        in_specs=specs,
        out_specs=jax.tree.map(lambda _: pl.BlockSpec(memory_space=pltpu.VMEM), outs),
        scratch_shapes=list(scratch),
        compiler_params=pltpu.CompilerParams(vmem_limit_bytes=56 << 20),
        interpret=INTERPRET,
        cost_estimate=cost,
    )(*args)


def transposed(weight):
    return weight.reshape(27, C, C).transpose(0, 2, 1).reshape(27 * C, C)


def ring(axes):
    count = lax.axis_size(axes)
    forward = [(i, i + 1) for i in range(count - 1)]
    return forward, [(b, a) for a, b in forward]


GXN = ("y_lo", "x", "z_hi", "z_lo")
GYN = ("y_hi", "core")
YX = ("y_hi", "y_lo", "x")


def exchange(x_faces, y_faces):
    forward, backward = ring(GXN)
    x_lo = lax.ppermute(x_faces[1], GXN, forward)
    x_hi = lax.ppermute(x_faces[0], GXN, backward)

    def face(y):
        at = (GY - 2) * GZ if y else 0
        ends = [end.reshape(2, 2, GY * GZ, C)[:, :, at : at + 2 * GZ] for end in (x_lo, x_hi)]
        return jnp.concatenate([ends[0], y_faces[y], ends[1]], axis=1)

    forward, backward = ring(GYN)
    y_lo = lax.ppermute(face(1), GYN, forward)
    y_hi = lax.ppermute(face(0), GYN, backward)
    return x_lo, x_hi, y_lo, y_hi


def swap(values, axes):
    return lax.all_to_all(values, axes, 0, 0, tiled=True)


def scatter_sum(values, axes):
    count = lax.axis_size(axes)
    return swap(values.reshape(count, -1, C), axes).astype(F32).sum(axis=0)


def gather(values, axes):
    return swap(jnp.broadcast_to(values, (lax.axis_size(axes), *values.shape)), axes)


def reduce_terms(scale, pairs):
    core = lax.axis_index("core").astype(jnp.int32)
    cross = [(0, 1), (1, 0)]
    sent = gram(scale, 1 - core, pairs, BF)
    got = lax.ppermute(sent, "core", cross)
    own = gram(scale, core, pairs, F32)
    share = (own + got.astype(F32)).astype(BF)
    share = scatter_sum(share, YX)
    rows = share.shape[0]
    padded = -(-rows // (8 * lax.axis_size("z_lo"))) * 8 * lax.axis_size("z_lo")
    share = jnp.pad(share, ((0, padded - rows), (0, 0)))
    share = scatter_sum(share, "z_lo").astype(BF)
    share = gather(share, "z_hi").astype(F32).sum(axis=0).astype(BF)
    share = gather(share, "z_lo").reshape(padded, C)[:rows]
    share = gather(share, YX).reshape(-1, C)
    other = lax.ppermute(share, "core", cross)
    first = core == 0
    return jnp.where(first, share, other).astype(F32), jnp.where(first, other, share).astype(F32)


def compute(features, cotangent, block_pos, weight_one, weight_two):
    total_rows = block_pos.shape[0] * 64 * lax.axis_size(NAMES)
    scale = float(total_rows) ** -0.5
    face_x = jax.ShapeDtypeStruct((2, FACE, C), BF)
    face_y = jax.ShapeDtypeStruct((2, GX, 2 * GZ, C), BF)
    grid, *faces = call(
        place_kernel,
        (jax.ShapeDtypeStruct((2, ROWS, C), BF), face_x, face_x, face_y, face_y),
        smem=1,
        args=(block_pos, features, cotangent),
    )
    halo = exchange(faces[:2], faces[2:])
    one_t, two_t = lax.optimization_barrier((transposed(weight_one), transposed(weight_two)))
    pad = pltpu.VMEM((PX, PY, GZ, C), BF)
    pairs = call(
        middle_kernel,
        jax.ShapeDtypeStruct((2, 2, EX, EY, GZ, C), BF),
        scratch=(pad, pad, pltpu.VMEM((PX, PY, GZ, 3 * C), BF), pltpu.VMEM((EXT_ROWS, C), F32)),
        args=(grid, *halo, weight_one, two_t),
    )
    output, input_grad = call(
        final_kernel,
        (jax.ShapeDtypeStruct(features.shape, BF), jax.ShapeDtypeStruct(features.shape, F32)),
        scratch=(pltpu.VMEM((EX, EY, GZ, 3 * C), BF),),
        smem=1,
        args=(block_pos, pairs, weight_two, one_t),
        cost=pl.CostEstimate(flops=2 * 2 * 27 * ROWS * C * C, transcendentals=0, bytes_accessed=24 << 20),
    )
    grad_one, grad_two = reduce_terms(scale, pairs)
    return output, input_grad, grad_one, grad_two


def solution(mesh):
    split = Mesh(mesh.devices.reshape(DIMS), NAMES)
    rows = P(NAMES, None)
    return jax.shard_map(
        compute,
        mesh=split,
        in_specs=(rows, rows, P(NAMES), P(), P()),
        out_specs=(rows, rows, P(), P()),
        check_vma=False,
    )
```

```python
import jax
import jax.numpy as jnp
from jax import lax
from jax.experimental import pallas as pl
from jax.experimental.pallas import tpu as pltpu
from jax.sharding import Mesh
from jax.sharding import PartitionSpec as P


SLOTS = 8
C = 128
GX, GY, GZ = 8, 8, 16
EX, EY = GX + 2, GY + 2
PX, PY = GX + 4, GY + 4
ROWS = GX * GY * GZ
EXT_ROWS = EX * EY * GZ
PAD_ROWS = PX * PY * GZ
FACE = 2 * GY * GZ
DIMS = (2, 4, 4, 4, 2, 2)
NAMES = ("y_lo", "x", "z_hi", "z_lo", "y_hi", "core")
INTERPRET = False
BF = jnp.bfloat16
F32 = jnp.float32


def grid_row(pos_ref, index):
    slot = index >> 6
    pos = jnp.full(index.shape, -1, jnp.int32)
    for s in range(SLOTS):
        pos = jnp.where(slot == s, pos_ref[s], pos)
    safe = jnp.maximum(pos, 0)
    bx = (safe >= 6).astype(jnp.int32)
    rest = safe - 6 * bx
    by = (rest >= 3).astype(jnp.int32)
    bz = rest - 3 * by
    vx = (index >> 4) & 3
    vy = (index >> 2) & 3
    vz = index & 3
    row = ((bx * 4 + vx) * GY + by * 4 + vy) * GZ + bz * 4 + vz
    return jnp.where(pos >= 0, row, -1)


def dot(a, b, dims=((1,), (0,))):
    return lax.dot_general(a, b, (dims, ((), ())), preferred_element_type=F32)


def place_kernel(pos_ref, feat_ref, cot_ref, grid_ref, xlo_ref, xhi_ref, ylo_ref, yhi_ref):
    target = grid_row(pos_ref, lax.broadcasted_iota(jnp.int32, (1, SLOTS * 64), 1))
    rows = lax.broadcasted_iota(jnp.int32, (ROWS, SLOTS * 64), 0)
    perm = (rows == target).astype(F32).astype(BF)
    mask = dot(perm, jnp.ones((SLOTS * 64, C), BF))
    z = lax.broadcasted_iota(jnp.int32, (ROWS, C), 0) & (GZ - 1)
    flags = jnp.where(z == 13, pltpu.roll(mask, 13, 0) + 2.0 * pltpu.roll(mask, 5, 0), 0.0)
    flags = jnp.where(z == 14, pltpu.roll(mask, 10, 0), flags)
    for field, ref in enumerate((feat_ref, cot_ref)):
        placed = dot(perm, ref[...])
        placed = (placed + flags if field == 0 else placed).astype(BF)
        grid_ref[field] = placed
        xlo_ref[field] = placed[:FACE]
        xhi_ref[field] = placed[ROWS - FACE :]
        columns = placed.reshape(GX, GY * GZ, C)
        ylo_ref[field] = columns[:, : 2 * GZ]
        yhi_ref[field] = columns[:, (GY - 2) * GZ :]


def z_shifts(field, flip=False):
    rows = field.shape[0]
    wide = field.astype(F32)
    before = pltpu.roll(wide, 1, 0).astype(BF)
    after = pltpu.roll(wide, rows - 1, 0).astype(BF)
    return jnp.concatenate([after, field, before] if flip else [before, field, after], axis=1)


def fill_pad(pad_ref, grid, x_lo, x_hi, y_lo, y_hi):
    pad_ref[2 : PX - 2, 2 : PY - 2] = grid.reshape(GX, GY, GZ, C)
    pad_ref[:2, 2 : PY - 2] = x_lo.reshape(2, GY, GZ, C)
    pad_ref[PX - 2 :, 2 : PY - 2] = x_hi.reshape(2, GY, GZ, C)
    pad_ref[:, :2] = y_lo.reshape(PX, 2, GZ, C)
    pad_ref[:, PY - 2 :] = y_hi.reshape(PX, 2, GZ, C)


def conv(shift_ref, w_ref, flip):
    nx, ny = shift_ref.shape[0] - 2, shift_ref.shape[1] - 2

    def weight(dx, dy):
        k = 3 * dx + dy
        at = 8 - k if flip else k
        return w_ref[at * 3 * C : (at + 1) * 3 * C, :]

    def product(x, y, mx, my, rhs):
        lhs = shift_ref[x : x + mx, y : y + my].reshape(mx * my * GZ, 3 * C)
        return dot(lhs, rhs).reshape(mx, my, GZ, rhs.shape[1])

    acc = product(2, 2, nx, ny, weight(2, 2))
    for dx in range(3):
        pair = product(dx, 0, nx, ny + 1, jnp.concatenate([weight(dx, 0), weight(dx, 1)], axis=1))
        acc = acc + pair[:, :ny, :, :C] + pair[:, 1:, :, C:]
    pair = product(0, 2, nx + 1, ny, jnp.concatenate([weight(0, 2), weight(1, 2)], axis=1))
    return acc + pair[:nx, :, :, :C] + pair[1:, :, :, C:]


def active_rows(field):
    both, middle = field[:, :, 13:14], field[:, :, 14:15]
    high = (both > 1.5).astype(F32)
    low = both - 2.0 * high
    z = lax.broadcasted_iota(jnp.int32, field.shape, 2)
    upper = jnp.where(z < 8, jnp.broadcast_to(middle, field.shape), jnp.broadcast_to(high, field.shape))
    mask = jnp.where(z < 4, jnp.broadcast_to(low, field.shape), upper)
    return jnp.where(z < 12, mask, 0.0)


def middle_kernel(
    scale, core_ref, grid_ref, xlo_ref, xhi_ref, ylo_ref, yhi_ref, w1_ref, w2t_ref,
    pairs_ref, other_ref, own_ref, padx_ref, padu_ref, shift_ref, pre_ref,
):
    fill_pad(padx_ref, grid_ref[0], xlo_ref[0], xhi_ref[0], ylo_ref[0], yhi_ref[0])
    fill_pad(padu_ref, grid_ref[1], xlo_ref[1], xhi_ref[1], ylo_ref[1], yhi_ref[1])
    pairs_ref[0, 0] = padx_ref[1 : PX - 1, 1 : PY - 1]
    pairs_ref[1, 1] = padu_ref[1 : PX - 1, 1 : PY - 1]
    shift_ref[...] = z_shifts(padx_ref[...].reshape(PAD_ROWS, C)).reshape(PX, PY, GZ, 3 * C)
    pre_ref[...] = conv(shift_ref, w1_ref, False).reshape(EXT_ROWS, C)
    shift_ref[...] = z_shifts(padu_ref[...].reshape(PAD_ROWS, C), True).reshape(PX, PY, GZ, 3 * C)
    back = conv(shift_ref, w2t_ref, True).reshape(EXT_ROWS, C)
    pre = pre_ref[...]
    mask = active_rows(padx_ref[1 : PX - 1, 1 : PY - 1].astype(F32)).reshape(EXT_ROWS, C)
    sig = jax.nn.sigmoid(pre)
    pairs_ref[1, 0] = (pre * sig * mask).astype(BF).reshape(EX, EY, GZ, C)
    pairs_ref[0, 1] = (back * (sig * (1.0 + pre * (1.0 - sig))) * mask).astype(BF).reshape(EX, EY, GZ, C)
    gram(scale, pairs_ref, 1 - core_ref[0], other_ref)
    gram(scale, pairs_ref, core_ref[0], own_ref)


def gram(scale, pairs_ref, which, term_ref):
    left = pairs_ref[which, 0, 1 : EX - 1, 1 : EY - 1].reshape(ROWS, C)
    lhs = z_shifts(left).T
    for first in range(0, 9, 2):
        ks = range(first, min(first + 2, 9))
        starts = [(2 - k // 3, 2 - k % 3) for k in ks]
        rhs = [pairs_ref[which, 1, x : x + GX, y : y + GY].reshape(ROWS, C) for x, y in starts]
        prod = dot(lhs, jnp.concatenate(rhs, axis=1)) * scale
        for n, k in enumerate(ks):
            term_ref[3 * k * C : 3 * (k + 1) * C, :] = prod[:, n * C : (n + 1) * C].astype(BF)


def final_kernel(pos_ref, pairs_ref, w2_ref, w1t_ref, out_ref, grad_ref, shift_ref):
    target = grid_row(pos_ref, lax.broadcasted_iota(jnp.int32, (SLOTS * 64, 1), 0))
    rows = lax.broadcasted_iota(jnp.int32, (SLOTS * 64, ROWS), 1)
    perm = (rows == target).astype(F32).astype(BF)
    for field, w_ref in enumerate((w2_ref, w1t_ref)):
        source = pairs_ref[1 - field, field].reshape(EXT_ROWS, C)
        shift_ref[...] = z_shifts(source, field == 1).reshape(EX, EY, GZ, 3 * C)
        straight = pairs_ref[field, field, 1 : EX - 1, 1 : EY - 1].reshape(ROWS, C)
        value = conv(shift_ref, w_ref, field == 1).reshape(ROWS, C) + straight.astype(F32)
        high = value.astype(BF)
        if field == 0:
            out_ref[...] = dot(perm, high).astype(BF)
        else:
            low = (value - high.astype(F32)).astype(BF)
            grad_ref[...] = dot(perm, high) + dot(perm, low)


def call(kernel, outs, scratch=(), smem=0, args=(), cost=None):
    specs = [pl.BlockSpec(memory_space=pltpu.SMEM)] * smem
    specs += [pl.BlockSpec(memory_space=pltpu.VMEM)] * (len(args) - smem)
    return pl.pallas_call(
        kernel,
        out_shape=outs,
        in_specs=specs,
        out_specs=jax.tree.map(lambda _: pl.BlockSpec(memory_space=pltpu.VMEM), outs),
        scratch_shapes=list(scratch),
        compiler_params=pltpu.CompilerParams(vmem_limit_bytes=56 << 20),
        interpret=INTERPRET,
        cost_estimate=cost,
    )(*args)


def transposed(weight):
    return weight.reshape(27, C, C).transpose(0, 2, 1).reshape(27 * C, C)


def ring(axes):
    count = lax.axis_size(axes)
    forward = [(i, i + 1) for i in range(count - 1)]
    return forward, [(b, a) for a, b in forward]


GXN = ("y_lo", "x", "z_hi", "z_lo")
GYN = ("y_hi", "core")
YX = ("y_hi", "y_lo", "x")


def exchange(x_faces, y_faces):
    forward, backward = ring(GXN)
    x_lo = lax.ppermute(x_faces[1], GXN, forward)
    x_hi = lax.ppermute(x_faces[0], GXN, backward)

    def face(y):
        at = (GY - 2) * GZ if y else 0
        ends = [end.reshape(2, 2, GY * GZ, C)[:, :, at : at + 2 * GZ] for end in (x_lo, x_hi)]
        return jnp.concatenate([ends[0], y_faces[y], ends[1]], axis=1)

    forward, backward = ring(GYN)
    y_lo = lax.ppermute(face(1), GYN, forward)
    y_hi = lax.ppermute(face(0), GYN, backward)
    return x_lo, x_hi, y_lo, y_hi


def swap(values, axes):
    return lax.all_to_all(values, axes, 0, 0, tiled=True)


def scatter_sum(values, axes):
    count = lax.axis_size(axes)
    return swap(values.reshape(count, -1, C), axes).astype(F32).sum(axis=0)


def gather(values, axes):
    return swap(jnp.broadcast_to(values, (lax.axis_size(axes), *values.shape)), axes)


def reduce_terms(core, own, other):
    cross = [(0, 1), (1, 0)]
    got = lax.ppermute(other, "core", cross)
    share = (own.astype(F32) + got.astype(F32)).astype(BF)
    share = scatter_sum(share, YX)
    rows = share.shape[0]
    padded = -(-rows // (8 * lax.axis_size("z_lo"))) * 8 * lax.axis_size("z_lo")
    share = jnp.pad(share, ((0, padded - rows), (0, 0)))
    share = scatter_sum(share, "z_lo")
    share = gather(share, "z_hi").sum(axis=0).astype(BF)
    share = gather(share, "z_lo").reshape(padded, C)[:rows]
    share = gather(share, YX).reshape(-1, C)
    other = lax.ppermute(share, "core", cross)
    first = core == 0
    return jnp.where(first, share, other).astype(F32), jnp.where(first, other, share).astype(F32)


def compute(features, cotangent, block_pos, weight_one, weight_two):
    total_rows = block_pos.shape[0] * 64 * lax.axis_size(NAMES)
    scale = float(total_rows) ** -0.5
    face_x = jax.ShapeDtypeStruct((2, FACE, C), BF)
    face_y = jax.ShapeDtypeStruct((2, GX, 2 * GZ, C), BF)
    grid, *faces = call(
        place_kernel,
        (jax.ShapeDtypeStruct((2, ROWS, C), BF), face_x, face_x, face_y, face_y),
        smem=1,
        args=(block_pos, features, cotangent),
    )
    halo = exchange(faces[:2], faces[2:])
    one_t, two_t = lax.optimization_barrier((transposed(weight_one), transposed(weight_two)))
    core = lax.axis_index("core").astype(jnp.int32)
    pad = pltpu.VMEM((PX, PY, GZ, C), BF)
    term = jax.ShapeDtypeStruct((27 * C, C), BF)
    pairs, other, own = call(
        lambda *refs: middle_kernel(scale, *refs),
        (jax.ShapeDtypeStruct((2, 2, EX, EY, GZ, C), BF), term, term),
        scratch=(pad, pad, pltpu.VMEM((PX, PY, GZ, 3 * C), BF), pltpu.VMEM((EXT_ROWS, C), F32)),
        smem=1,
        args=(core.reshape(1), grid, *halo, weight_one, two_t),
    )
    output, input_grad = call(
        final_kernel,
        (jax.ShapeDtypeStruct(features.shape, BF), jax.ShapeDtypeStruct(features.shape, F32)),
        scratch=(pltpu.VMEM((EX, EY, GZ, 3 * C), BF),),
        smem=1,
        args=(block_pos, pairs, weight_two, one_t),
        cost=pl.CostEstimate(flops=2 * 2 * 27 * ROWS * C * C, transcendentals=0, bytes_accessed=24 << 20),
    )
    grad_one, grad_two = reduce_terms(core, own, other)
    return output, input_grad, grad_one, grad_two


def solution(mesh):
    split = Mesh(mesh.devices.reshape(DIMS), NAMES)
    rows = P(NAMES, None)
    return jax.shard_map(
        compute,
        mesh=split,
        in_specs=(rows, rows, P(NAMES), P(), P()),
        out_specs=(rows, rows, P(), P()),
        check_vma=False,
    )
```

```python
import jax
import jax.numpy as jnp
from jax import lax
from jax.experimental import pallas as pl
from jax.experimental.pallas import tpu as pltpu
from jax.sharding import Mesh
from jax.sharding import PartitionSpec as P


SLOTS = 8
C = 128
GX, GY, GZ = 8, 8, 16
EX, EY = GX + 2, GY + 2
PX, PY = GX + 4, GY + 4
ROWS = GX * GY * GZ
EXT_ROWS = EX * EY * GZ
PAD_ROWS = PX * PY * GZ
FACE = 2 * GY * GZ
DIMS = (2, 4, 4, 4, 2, 2)
NAMES = ("y_lo", "x", "z_hi", "z_lo", "y_hi", "core")
INTERPRET = False
BF = jnp.bfloat16
F32 = jnp.float32


def grid_row(pos_ref, index):
    slot = index >> 6
    pos = jnp.full(index.shape, -1, jnp.int32)
    for s in range(SLOTS):
        pos = jnp.where(slot == s, pos_ref[s], pos)
    safe = jnp.maximum(pos, 0)
    bx = (safe >= 6).astype(jnp.int32)
    rest = safe - 6 * bx
    by = (rest >= 3).astype(jnp.int32)
    bz = rest - 3 * by
    vx = (index >> 4) & 3
    vy = (index >> 2) & 3
    vz = index & 3
    row = ((bx * 4 + vx) * GY + by * 4 + vy) * GZ + bz * 4 + vz
    return jnp.where(pos >= 0, row, -1)


def dot(a, b, dims=((1,), (0,))):
    return lax.dot_general(a, b, (dims, ((), ())), preferred_element_type=F32)


def place_kernel(pos_ref, feat_ref, cot_ref, grid_ref, xlo_ref, xhi_ref, ylo_ref, yhi_ref):
    target = grid_row(pos_ref, lax.broadcasted_iota(jnp.int32, (1, SLOTS * 64), 1))
    rows = lax.broadcasted_iota(jnp.int32, (ROWS, SLOTS * 64), 0)
    perm = (rows == target).astype(F32).astype(BF)
    mask = dot(perm, jnp.ones((SLOTS * 64, C), BF))
    z = lax.broadcasted_iota(jnp.int32, (ROWS, C), 0) & (GZ - 1)
    flags = jnp.where(z == 13, pltpu.roll(mask, 13, 0) + 2.0 * pltpu.roll(mask, 5, 0), 0.0)
    flags = jnp.where(z == 14, pltpu.roll(mask, 10, 0), flags)
    for field, ref in enumerate((feat_ref, cot_ref)):
        placed = dot(perm, ref[...])
        placed = (placed + flags if field == 0 else placed).astype(BF)
        grid_ref[field] = placed
        xlo_ref[field] = placed[:FACE]
        xhi_ref[field] = placed[ROWS - FACE :]
        columns = placed.reshape(GX, GY * GZ, C)
        ylo_ref[field] = columns[:, : 2 * GZ]
        yhi_ref[field] = columns[:, (GY - 2) * GZ :]


def z_shifts(field, flip=False):
    rows = field.shape[0]
    wide = field.astype(F32)
    before = pltpu.roll(wide, 1, 0).astype(BF)
    after = pltpu.roll(wide, rows - 1, 0).astype(BF)
    return jnp.concatenate([after, field, before] if flip else [before, field, after], axis=1)


def fill_pad(pad_ref, grid, x_lo, x_hi, y_lo, y_hi):
    pad_ref[2 : PX - 2, 2 : PY - 2] = grid.reshape(GX, GY, GZ, C)
    pad_ref[:2, 2 : PY - 2] = x_lo.reshape(2, GY, GZ, C)
    pad_ref[PX - 2 :, 2 : PY - 2] = x_hi.reshape(2, GY, GZ, C)
    pad_ref[:, :2] = y_lo.reshape(PX, 2, GZ, C)
    pad_ref[:, PY - 2 :] = y_hi.reshape(PX, 2, GZ, C)


def conv(shift_ref, w_ref, flip):
    nx, ny = shift_ref.shape[0] - 2, shift_ref.shape[1] - 2

    def weight(dx, dy):
        k = 3 * dx + dy
        at = 8 - k if flip else k
        return w_ref[at * 3 * C : (at + 1) * 3 * C, :]

    def product(x, y, mx, my, rhs):
        lhs = shift_ref[x : x + mx, y : y + my].reshape(mx * my * GZ, 3 * C)
        return dot(lhs, rhs).reshape(mx, my, GZ, rhs.shape[1])

    acc = product(2, 2, nx, ny, weight(2, 2))
    for dx in range(3):
        pair = product(dx, 0, nx, ny + 1, jnp.concatenate([weight(dx, 0), weight(dx, 1)], axis=1))
        acc = acc + pair[:, :ny, :, :C] + pair[:, 1:, :, C:]
    pair = product(0, 2, nx + 1, ny, jnp.concatenate([weight(0, 2), weight(1, 2)], axis=1))
    return acc + pair[:nx, :, :, :C] + pair[1:, :, :, C:]


def active_rows(field):
    both, middle = field[:, :, 13:14], field[:, :, 14:15]
    high = (both > 1.5).astype(F32)
    low = both - 2.0 * high
    z = lax.broadcasted_iota(jnp.int32, field.shape, 2)
    upper = jnp.where(z < 8, jnp.broadcast_to(middle, field.shape), jnp.broadcast_to(high, field.shape))
    mask = jnp.where(z < 4, jnp.broadcast_to(low, field.shape), upper)
    return jnp.where(z < 12, mask, 0.0)


def middle_kernel(
    scale, core_ref, grid_ref, xlo_ref, xhi_ref, ylo_ref, yhi_ref, w1_any, w2t_any,
    pairs_any, other_any, own_any,
    padx_ref, padu_ref, shift_ref, pre_ref, w1_ref, w2t_ref, pairs_ref, other_ref, own_ref, sems,
):
    first_in = pltpu.make_async_copy(w1_any, w1_ref, sems.at[0])
    second_in = pltpu.make_async_copy(w2t_any, w2t_ref, sems.at[1])
    first_in.start()
    second_in.start()
    fill_pad(padx_ref, grid_ref[0], xlo_ref[0], xhi_ref[0], ylo_ref[0], yhi_ref[0])
    fill_pad(padu_ref, grid_ref[1], xlo_ref[1], xhi_ref[1], ylo_ref[1], yhi_ref[1])
    pairs_ref[0, 0] = padx_ref[1 : PX - 1, 1 : PY - 1]
    pairs_ref[1, 1] = padu_ref[1 : PX - 1, 1 : PY - 1]
    shift_ref[...] = z_shifts(padx_ref[...].reshape(PAD_ROWS, C)).reshape(PX, PY, GZ, 3 * C)
    first_in.wait()
    pre_ref[...] = conv(shift_ref, w1_ref, False).reshape(EXT_ROWS, C)
    shift_ref[...] = z_shifts(padu_ref[...].reshape(PAD_ROWS, C), True).reshape(PX, PY, GZ, 3 * C)
    second_in.wait()
    back = conv(shift_ref, w2t_ref, True).reshape(EXT_ROWS, C)
    pre = pre_ref[...]
    mask = active_rows(padx_ref[1 : PX - 1, 1 : PY - 1].astype(F32)).reshape(EXT_ROWS, C)
    sig = jax.nn.sigmoid(pre)
    pairs_ref[1, 0] = (pre * sig * mask).astype(BF).reshape(EX, EY, GZ, C)
    pairs_ref[0, 1] = (back * (sig * (1.0 + pre * (1.0 - sig))) * mask).astype(BF).reshape(EX, EY, GZ, C)
    pairs_out = pltpu.make_async_copy(pairs_ref, pairs_any, sems.at[2])
    pairs_out.start()
    gram(scale, pairs_ref, 1 - core_ref[0], other_ref)
    other_out = pltpu.make_async_copy(other_ref, other_any, sems.at[3])
    other_out.start()
    gram(scale, pairs_ref, core_ref[0], own_ref)
    own_out = pltpu.make_async_copy(own_ref, own_any, sems.at[4])
    own_out.start()
    pairs_out.wait()
    other_out.wait()
    own_out.wait()


def gram(scale, pairs_ref, which, term_ref):
    left = pairs_ref[which, 0, 1 : EX - 1, 1 : EY - 1].reshape(ROWS, C)
    lhs = z_shifts(left).T
    for first in range(0, 9, 2):
        ks = range(first, min(first + 2, 9))
        starts = [(2 - k // 3, 2 - k % 3) for k in ks]
        rhs = [pairs_ref[which, 1, x : x + GX, y : y + GY].reshape(ROWS, C) for x, y in starts]
        prod = dot(lhs, jnp.concatenate(rhs, axis=1)) * scale
        for n, k in enumerate(ks):
            term_ref[3 * k * C : 3 * (k + 1) * C, :] = prod[:, n * C : (n + 1) * C].astype(BF)


def final_kernel(pos_ref, pairs_ref, w2_ref, w1t_ref, out_ref, grad_ref, shift_ref):
    target = grid_row(pos_ref, lax.broadcasted_iota(jnp.int32, (SLOTS * 64, 1), 0))
    rows = lax.broadcasted_iota(jnp.int32, (SLOTS * 64, ROWS), 1)
    perm = (rows == target).astype(F32).astype(BF)
    for field, w_ref in enumerate((w2_ref, w1t_ref)):
        source = pairs_ref[1 - field, field].reshape(EXT_ROWS, C)
        shift_ref[...] = z_shifts(source, field == 1).reshape(EX, EY, GZ, 3 * C)
        straight = pairs_ref[field, field, 1 : EX - 1, 1 : EY - 1].reshape(ROWS, C)
        value = conv(shift_ref, w_ref, field == 1).reshape(ROWS, C) + straight.astype(F32)
        high = value.astype(BF)
        if field == 0:
            out_ref[...] = dot(perm, high).astype(BF)
        else:
            low = (value - high.astype(F32)).astype(BF)
            grad_ref[...] = dot(perm, high) + dot(perm, low)


def call(kernel, outs, scratch=(), smem=0, args=(), cost=None, manual=0):
    specs = [pl.BlockSpec(memory_space=pltpu.SMEM)] * smem
    specs += [pl.BlockSpec(memory_space=pltpu.VMEM)] * (len(args) - smem - manual)
    specs += [pl.BlockSpec(memory_space=pl.ANY)] * manual
    out_space = pl.ANY if manual else pltpu.VMEM
    return pl.pallas_call(
        kernel,
        out_shape=outs,
        in_specs=specs,
        out_specs=jax.tree.map(lambda _: pl.BlockSpec(memory_space=out_space), outs),
        scratch_shapes=list(scratch),
        compiler_params=pltpu.CompilerParams(vmem_limit_bytes=56 << 20),
        interpret=INTERPRET,
        cost_estimate=cost,
    )(*args)


def transposed(weight):
    return weight.reshape(27, C, C).transpose(0, 2, 1).reshape(27 * C, C)


def ring(axes):
    count = lax.axis_size(axes)
    forward = [(i, i + 1) for i in range(count - 1)]
    return forward, [(b, a) for a, b in forward]


GXN = ("y_lo", "x", "z_hi", "z_lo")
GYN = ("y_hi", "core")
YX = ("y_hi", "y_lo", "x")


def exchange(x_faces, y_faces):
    forward, backward = ring(GXN)
    x_lo = lax.ppermute(x_faces[1], GXN, forward)
    x_hi = lax.ppermute(x_faces[0], GXN, backward)

    def face(y):
        at = (GY - 2) * GZ if y else 0
        ends = [end.reshape(2, 2, GY * GZ, C)[:, :, at : at + 2 * GZ] for end in (x_lo, x_hi)]
        return jnp.concatenate([ends[0], y_faces[y], ends[1]], axis=1)

    forward, backward = ring(GYN)
    y_lo = lax.ppermute(face(1), GYN, forward)
    y_hi = lax.ppermute(face(0), GYN, backward)
    return x_lo, x_hi, y_lo, y_hi


def swap(values, axes):
    return lax.all_to_all(values, axes, 0, 0, tiled=True)


def scatter_sum(values, axes):
    count = lax.axis_size(axes)
    return swap(values.reshape(count, -1, C), axes).astype(F32).sum(axis=0)


def gather(values, axes):
    return swap(jnp.broadcast_to(values, (lax.axis_size(axes), *values.shape)), axes)


def reduce_terms(core, own, other):
    cross = [(0, 1), (1, 0)]
    got = lax.ppermute(other, "core", cross)
    share = (own.astype(F32) + got.astype(F32)).astype(BF)
    share = scatter_sum(share, YX)
    rows = share.shape[0]
    padded = -(-rows // (8 * lax.axis_size("z_lo"))) * 8 * lax.axis_size("z_lo")
    share = jnp.pad(share, ((0, padded - rows), (0, 0)))
    share = scatter_sum(share, "z_lo")
    share = gather(share, "z_hi").sum(axis=0).astype(BF)
    share = gather(share, "z_lo").reshape(padded, C)[:rows]
    share = gather(share, YX).reshape(-1, C)
    other = lax.ppermute(share, "core", cross)
    first = core == 0
    return jnp.where(first, share, other).astype(F32), jnp.where(first, other, share).astype(F32)


def compute(features, cotangent, block_pos, weight_one, weight_two):
    total_rows = block_pos.shape[0] * 64 * lax.axis_size(NAMES)
    scale = float(total_rows) ** -0.5
    face_x = jax.ShapeDtypeStruct((2, FACE, C), BF)
    face_y = jax.ShapeDtypeStruct((2, GX, 2 * GZ, C), BF)
    grid, *faces = call(
        place_kernel,
        (jax.ShapeDtypeStruct((2, ROWS, C), BF), face_x, face_x, face_y, face_y),
        smem=1,
        args=(block_pos, features, cotangent),
    )
    halo = exchange(faces[:2], faces[2:])
    one_t, two_t = lax.optimization_barrier((transposed(weight_one), transposed(weight_two)))
    core = lax.axis_index("core").astype(jnp.int32)
    pad = pltpu.VMEM((PX, PY, GZ, C), BF)
    term = jax.ShapeDtypeStruct((27 * C, C), BF)
    block = pltpu.VMEM((27 * C, C), BF)
    pairs, other, own = call(
        lambda *refs: middle_kernel(scale, *refs),
        (jax.ShapeDtypeStruct((2, 2, EX, EY, GZ, C), BF), term, term),
        scratch=(
            pad, pad, pltpu.VMEM((PX, PY, GZ, 3 * C), BF), pltpu.VMEM((EXT_ROWS, C), F32),
            block, block, pltpu.VMEM((2, 2, EX, EY, GZ, C), BF), block, block, pltpu.SemaphoreType.DMA((5,)),
        ),
        smem=1,
        manual=2,
        args=(core.reshape(1), grid, *halo, weight_one, two_t),
    )
    output, input_grad = call(
        final_kernel,
        (jax.ShapeDtypeStruct(features.shape, BF), jax.ShapeDtypeStruct(features.shape, F32)),
        scratch=(pltpu.VMEM((EX, EY, GZ, 3 * C), BF),),
        smem=1,
        args=(block_pos, pairs, weight_two, one_t),
        cost=pl.CostEstimate(flops=2 * 2 * 27 * ROWS * C * C, transcendentals=0, bytes_accessed=24 << 20),
    )
    grad_one, grad_two = reduce_terms(core, own, other)
    return output, input_grad, grad_one, grad_two


def solution(mesh):
    split = Mesh(mesh.devices.reshape(DIMS), NAMES)
    rows = P(NAMES, None)
    return jax.shard_map(
        compute,
        mesh=split,
        in_specs=(rows, rows, P(NAMES), P(), P()),
        out_specs=(rows, rows, P(), P()),
        check_vma=False,
    )
```

```python
import jax
import jax.numpy as jnp
from jax import lax
from jax.experimental import pallas as pl
from jax.experimental.pallas import tpu as pltpu
from jax.sharding import Mesh
from jax.sharding import PartitionSpec as P


SLOTS = 8
C = 128
GX, GY, GZ = 8, 8, 16
EX, EY = GX + 2, GY + 2
PX, PY = GX + 4, GY + 4
ROWS = GX * GY * GZ
EXT_ROWS = EX * EY * GZ
PAD_ROWS = PX * PY * GZ
FACE = 2 * GY * GZ
DIMS = (2, 4, 4, 4, 2, 2)
NAMES = ("y_lo", "x", "z_hi", "z_lo", "y_hi", "core")
INTERPRET = False
BF = jnp.bfloat16
F32 = jnp.float32


def grid_row(pos_ref, index):
    slot = index >> 6
    pos = jnp.full(index.shape, -1, jnp.int32)
    for s in range(SLOTS):
        pos = jnp.where(slot == s, pos_ref[s], pos)
    safe = jnp.maximum(pos, 0)
    bx = (safe >= 6).astype(jnp.int32)
    rest = safe - 6 * bx
    by = (rest >= 3).astype(jnp.int32)
    bz = rest - 3 * by
    vx = (index >> 4) & 3
    vy = (index >> 2) & 3
    vz = index & 3
    row = ((bx * 4 + vx) * GY + by * 4 + vy) * GZ + bz * 4 + vz
    return jnp.where(pos >= 0, row, -1)


def dot(a, b, dims=((1,), (0,))):
    return lax.dot_general(a, b, (dims, ((), ())), preferred_element_type=F32)


def place_kernel(pos_ref, feat_ref, cot_ref, grid_ref, xlo_ref, xhi_ref, ylo_ref, yhi_ref):
    target = grid_row(pos_ref, lax.broadcasted_iota(jnp.int32, (1, SLOTS * 64), 1))
    rows = lax.broadcasted_iota(jnp.int32, (ROWS, SLOTS * 64), 0)
    perm = (rows == target).astype(F32).astype(BF)
    mask = dot(perm, jnp.ones((SLOTS * 64, C), BF))
    z = lax.broadcasted_iota(jnp.int32, (ROWS, C), 0) & (GZ - 1)
    flags = jnp.where(z == 13, pltpu.roll(mask, 13, 0) + 2.0 * pltpu.roll(mask, 5, 0), 0.0)
    flags = jnp.where(z == 14, pltpu.roll(mask, 10, 0), flags)
    for field, ref in enumerate((feat_ref, cot_ref)):
        placed = dot(perm, ref[...])
        placed = (placed + flags if field == 0 else placed).astype(BF)
        grid_ref[field] = placed
        xlo_ref[field] = placed[:FACE]
        xhi_ref[field] = placed[ROWS - FACE :]
        columns = placed.reshape(GX, GY * GZ, C)
        ylo_ref[field] = columns[:, : 2 * GZ]
        yhi_ref[field] = columns[:, (GY - 2) * GZ :]


def z_shifts(field, flip=False):
    rows = field.shape[0]
    wide = field.astype(F32)
    before = pltpu.roll(wide, 1, 0).astype(BF)
    after = pltpu.roll(wide, rows - 1, 0).astype(BF)
    return jnp.concatenate([after, field, before] if flip else [before, field, after], axis=1)


def fill_pad(pad_ref, grid, x_lo, x_hi, y_lo, y_hi):
    pad_ref[2 : PX - 2, 2 : PY - 2] = grid.reshape(GX, GY, GZ, C)
    pad_ref[:2, 2 : PY - 2] = x_lo.reshape(2, GY, GZ, C)
    pad_ref[PX - 2 :, 2 : PY - 2] = x_hi.reshape(2, GY, GZ, C)
    pad_ref[:, :2] = y_lo.reshape(PX, 2, GZ, C)
    pad_ref[:, PY - 2 :] = y_hi.reshape(PX, 2, GZ, C)


def conv(shift_ref, w_ref, flip):
    nx, ny = shift_ref.shape[0] - 2, shift_ref.shape[1] - 2

    def weight(dx, dy):
        k = 3 * dx + dy
        at = 8 - k if flip else k
        return w_ref[at * 3 * C : (at + 1) * 3 * C, :]

    def product(x, y, mx, my, rhs):
        lhs = shift_ref[x : x + mx, y : y + my].reshape(mx * my * GZ, 3 * C)
        return dot(lhs, rhs).reshape(mx, my, GZ, rhs.shape[1])

    acc = product(2, 2, nx, ny, weight(2, 2))
    for dx in range(3):
        pair = product(dx, 0, nx, ny + 1, jnp.concatenate([weight(dx, 0), weight(dx, 1)], axis=1))
        acc = acc + pair[:, :ny, :, :C] + pair[:, 1:, :, C:]
    pair = product(0, 2, nx + 1, ny, jnp.concatenate([weight(0, 2), weight(1, 2)], axis=1))
    return acc + pair[:nx, :, :, :C] + pair[1:, :, :, C:]


def active_rows(field):
    both, middle = field[:, :, 13:14], field[:, :, 14:15]
    high = (both > 1.5).astype(F32)
    low = both - 2.0 * high
    z = lax.broadcasted_iota(jnp.int32, field.shape, 2)
    upper = jnp.where(z < 8, jnp.broadcast_to(middle, field.shape), jnp.broadcast_to(high, field.shape))
    mask = jnp.where(z < 4, jnp.broadcast_to(low, field.shape), upper)
    return jnp.where(z < 12, mask, 0.0)


def middle_kernel(
    scale, core_ref, grid_ref, xlo_ref, xhi_ref, ylo_ref, yhi_ref, w1_ref, w2t_ref,
    pairs_ref, other_ref, own_ref, padx_ref, padu_ref, shift_ref, pre_ref,
):
    fill_pad(padx_ref, grid_ref[0], xlo_ref[0], xhi_ref[0], ylo_ref[0], yhi_ref[0])
    fill_pad(padu_ref, grid_ref[1], xlo_ref[1], xhi_ref[1], ylo_ref[1], yhi_ref[1])
    pairs_ref[0, 0] = padx_ref[1 : PX - 1, 1 : PY - 1]
    pairs_ref[1, 1] = padu_ref[1 : PX - 1, 1 : PY - 1]
    shift_ref[...] = z_shifts(padx_ref[...].reshape(PAD_ROWS, C)).reshape(PX, PY, GZ, 3 * C)
    pre_ref[...] = conv(shift_ref, w1_ref, False).reshape(EXT_ROWS, C)
    shift_ref[...] = z_shifts(padu_ref[...].reshape(PAD_ROWS, C), True).reshape(PX, PY, GZ, 3 * C)
    back = conv(shift_ref, w2t_ref, True).reshape(EXT_ROWS, C)
    pre = pre_ref[...]
    mask = active_rows(padx_ref[1 : PX - 1, 1 : PY - 1].astype(F32)).reshape(EXT_ROWS, C)
    sig = jax.nn.sigmoid(pre)
    pairs_ref[1, 0] = (pre * sig * mask).astype(BF).reshape(EX, EY, GZ, C)
    pairs_ref[0, 1] = (back * (sig * (1.0 + pre * (1.0 - sig))) * mask).astype(BF).reshape(EX, EY, GZ, C)
    gram(scale, pairs_ref, 1 - core_ref[0], other_ref)
    gram(scale, pairs_ref, core_ref[0], own_ref)


def gram(scale, pairs_ref, which, term_ref):
    left = pairs_ref[which, 0, 1 : EX - 1, 1 : EY - 1].reshape(ROWS, C)
    lhs = z_shifts(left).T
    for first in range(0, 9, 2):
        ks = range(first, min(first + 2, 9))
        starts = [(2 - k // 3, 2 - k % 3) for k in ks]
        rhs = [pairs_ref[which, 1, x : x + GX, y : y + GY].reshape(ROWS, C) for x, y in starts]
        prod = dot(lhs, jnp.concatenate(rhs, axis=1)) * scale
        for n, k in enumerate(ks):
            term_ref[3 * k * C : 3 * (k + 1) * C, :] = prod[:, n * C : (n + 1) * C].astype(BF)


def final_kernel(pos_ref, pairs_ref, w2_ref, w1t_ref, out_ref, grad_ref, shift_ref):
    target = grid_row(pos_ref, lax.broadcasted_iota(jnp.int32, (SLOTS * 64, 1), 0))
    rows = lax.broadcasted_iota(jnp.int32, (SLOTS * 64, ROWS), 1)
    perm = (rows == target).astype(F32).astype(BF)
    for field, w_ref in enumerate((w2_ref, w1t_ref)):
        source = pairs_ref[1 - field, field].reshape(EXT_ROWS, C)
        shift_ref[...] = z_shifts(source, field == 1).reshape(EX, EY, GZ, 3 * C)
        straight = pairs_ref[field, field, 1 : EX - 1, 1 : EY - 1].reshape(ROWS, C)
        value = conv(shift_ref, w_ref, field == 1).reshape(ROWS, C) + straight.astype(F32)
        high = value.astype(BF)
        if field == 0:
            out_ref[...] = dot(perm, high).astype(BF)
        else:
            low = (value - high.astype(F32)).astype(BF)
            grad_ref[...] = dot(perm, high) + dot(perm, low)


def call(kernel, outs, scratch=(), smem=0, args=(), cost=None):
    specs = [pl.BlockSpec(memory_space=pltpu.SMEM)] * smem
    specs += [pl.BlockSpec(memory_space=pltpu.VMEM)] * (len(args) - smem)
    return pl.pallas_call(
        kernel,
        out_shape=outs,
        in_specs=specs,
        out_specs=jax.tree.map(lambda _: pl.BlockSpec(memory_space=pltpu.VMEM), outs),
        scratch_shapes=list(scratch),
        compiler_params=pltpu.CompilerParams(vmem_limit_bytes=56 << 20),
        interpret=INTERPRET,
        cost_estimate=cost,
    )(*args)


def transposed(weight):
    return weight.reshape(27, C, C).transpose(0, 2, 1).reshape(27 * C, C)


def ring(axes):
    count = lax.axis_size(axes)
    forward = [(i, i + 1) for i in range(count - 1)]
    return forward, [(b, a) for a, b in forward]


GXN = ("y_lo", "x", "z_hi", "z_lo")
GYN = ("y_hi", "core")
YX = ("y_hi", "y_lo", "x")
Z = ("z_hi", "z_lo")


def exchange(x_faces, y_faces):
    forward, backward = ring(GXN)
    x_lo = lax.ppermute(x_faces[1], GXN, forward)
    x_hi = lax.ppermute(x_faces[0], GXN, backward)

    def face(y):
        at = (GY - 2) * GZ if y else 0
        ends = [end.reshape(2, 2, GY * GZ, C)[:, :, at : at + 2 * GZ] for end in (x_lo, x_hi)]
        return jnp.concatenate([ends[0], y_faces[y], ends[1]], axis=1)

    forward, backward = ring(GYN)
    y_lo = lax.ppermute(face(1), GYN, forward)
    y_hi = lax.ppermute(face(0), GYN, backward)
    return x_lo, x_hi, y_lo, y_hi


def swap(values, axes):
    return lax.all_to_all(values, axes, 0, 0, tiled=True)


def scatter_sum(values, axes):
    count = lax.axis_size(axes)
    return swap(values.reshape(count, -1, C), axes).astype(F32).sum(axis=0)


def gather(values, axes):
    return swap(jnp.broadcast_to(values, (lax.axis_size(axes), *values.shape)), axes)


def reduce_terms(core, own, other):
    cross = [(0, 1), (1, 0)]
    got = lax.ppermute(other, "core", cross)
    share = (own.astype(F32) + got.astype(F32)).astype(BF)
    share = scatter_sum(share, YX)
    rows = share.shape[0]
    padded = -(-rows // (8 * lax.axis_size(Z))) * 8 * lax.axis_size(Z)
    share = jnp.pad(share, ((0, padded - rows), (0, 0))).astype(BF)
    share = scatter_sum(share, Z).astype(BF)
    share = gather(share, Z).reshape(padded, C)[:rows]
    share = gather(share, YX).reshape(-1, C)
    other = lax.ppermute(share, "core", cross)
    first = core == 0
    return jnp.where(first, share, other).astype(F32), jnp.where(first, other, share).astype(F32)


def compute(features, cotangent, block_pos, weight_one, weight_two):
    total_rows = block_pos.shape[0] * 64 * lax.axis_size(NAMES)
    scale = float(total_rows) ** -0.5
    face_x = jax.ShapeDtypeStruct((2, FACE, C), BF)
    face_y = jax.ShapeDtypeStruct((2, GX, 2 * GZ, C), BF)
    grid, *faces = call(
        place_kernel,
        (jax.ShapeDtypeStruct((2, ROWS, C), BF), face_x, face_x, face_y, face_y),
        smem=1,
        args=(block_pos, features, cotangent),
    )
    halo = exchange(faces[:2], faces[2:])
    one_t, two_t = lax.optimization_barrier((transposed(weight_one), transposed(weight_two)))
    core = lax.axis_index("core").astype(jnp.int32)
    pad = pltpu.VMEM((PX, PY, GZ, C), BF)
    term = jax.ShapeDtypeStruct((27 * C, C), BF)
    pairs, other, own = call(
        lambda *refs: middle_kernel(scale, *refs),
        (jax.ShapeDtypeStruct((2, 2, EX, EY, GZ, C), BF), term, term),
        scratch=(pad, pad, pltpu.VMEM((PX, PY, GZ, 3 * C), BF), pltpu.VMEM((EXT_ROWS, C), F32)),
        smem=1,
        args=(core.reshape(1), grid, *halo, weight_one, two_t),
    )
    output, input_grad = call(
        final_kernel,
        (jax.ShapeDtypeStruct(features.shape, BF), jax.ShapeDtypeStruct(features.shape, F32)),
        scratch=(pltpu.VMEM((EX, EY, GZ, 3 * C), BF),),
        smem=1,
        args=(block_pos, pairs, weight_two, one_t),
        cost=pl.CostEstimate(flops=2 * 2 * 27 * ROWS * C * C, transcendentals=0, bytes_accessed=24 << 20),
    )
    grad_one, grad_two = reduce_terms(core, own, other)
    return output, input_grad, grad_one, grad_two


def solution(mesh):
    split = Mesh(mesh.devices.reshape(DIMS), NAMES)
    rows = P(NAMES, None)
    return jax.shard_map(
        compute,
        mesh=split,
        in_specs=(rows, rows, P(NAMES), P(), P()),
        out_specs=(rows, rows, P(), P()),
        check_vma=False,
    )
```
